32 devices in a mesh: sample: 8 (over y, x, core), chan: 4 (over z).
Axes of the slice: x: 2, y: 2, z: 4, core: 2. Of those that a mesh axis runs over, the one named last changes fastest.
Arguments:
- snapshots: bfloat16 [8, 256, 512], P('sample', None, 'chan'), may hold values from -6 to 6
- first_weight: bfloat16 [256, 27, 256], P('chan'), may hold values from -0.078125 to 0.078125
- second_weight: bfloat16 [256, 27, 256], P('chan'), may hold values from -0.078125 to 0.078125
- cotangent: bfloat16 [8, 256, 512], P('sample', 'chan'), may hold values from -0.09375 to 0.09375
Outputs:
- second_out: bfloat16 [8, 256, 512], P('sample', 'chan')
- first_grad: float32 [256, 27, 256], P('chan', None, 'sample')
- second_grad: float32 [256, 27, 256], P('chan', None, 'sample')
The draws below stay inside these ranges and needn't reach their ends.
All inputs are finite; a program needn't handle non-finite values.
Results may differ from the reference program's by a relative error of at most 0.0061.
Values may be sent and summed in bfloat16 or wider, within the bound.
No kernel may reach another device: no remote copies, remote signals or barrier semaphores. Data moves between devices by JAX's collectives and lax.ppermute only.
A program may use at most 128 MiB of HBM per device.

```python
import jax
import jax.numpy as jnp
from jax import lax

CH = 256
SIDE = 8
TAPS = 27
CELLS = 512
NB = 8


def levels(stream_key, extent, shards, least, high):
    factor_of = 1.0
    for dim, shards_of in shards:
        steps = jax.random.uniform(jax.random.fold_in(jax.random.fold_in(stream_key, 6), dim), (shards_of,), jnp.float32, least / len(shards), high / len(shards))
        factor_of = factor_of * jnp.repeat(jnp.exp(steps), extent[dim] // shards_of).reshape((-1,) + (1,) * (len(extent) - 1 - dim))
    return factor_of


def bell_draw(key, extent, scale, most, shards=(), dtype=jnp.bfloat16):
    entries = jax.random.normal(key, extent, jnp.float32) * scale
    if len(shards) > 0:
        entries = levels(key, extent, shards, -0.22, 0.18) * entries
    return jnp.clip(entries, min=-most, max=most).astype(dtype)


def setup_inputs(seed: int = 0) -> dict:
    seeds = jax.random.split(jax.random.key(seed), 5)
    snapshots = bell_draw(seeds[0], (NB, CH, CELLS), 1.0, 6.0, ((0, 8), (2, 4)))
    first_weight = bell_draw(seeds[1], (CH, TAPS, CH), (CH * TAPS) ** -0.5, 0.078125, ((0, 4),))
    second_weight = bell_draw(seeds[2], (CH, TAPS, CH), (CH * TAPS) ** -0.5, 0.078125, ((0, 4),))
    cotangent = bell_draw(seeds[3], (NB, CH, CELLS), (1.0 / (SIDE * SIDE)), 0.09375, ((0, 8), (1, 4)))
    return dict(snapshots=snapshots, first_weight=first_weight, second_weight=second_weight, cotangent=cotangent)


def shifted(fields):
    batch_size, channels = fields.shape[0], fields.shape[1]
    cube_form = fields.reshape(batch_size, channels, SIDE, SIDE, SIDE)
    padded = jnp.pad(cube_form, ((0, 0), (0, 0), (1, 1), (1, 1), (1, 1)))
    shifted_views = []
    for tap_index in range(27):
        shift_depth, shift_rows, shift_cols = tap_index // 9, (tap_index // 3) % 3, tap_index % 3
        shifted_views.append(padded[:, :, shift_depth:shift_depth + SIDE, shift_rows:shift_rows + SIDE, shift_cols:shift_cols + SIDE])
    return jnp.stack(shifted_views, axis=2).reshape(batch_size, channels * 27, SIDE * SIDE * SIDE)


def spread(terms):
    batch_size, channels = terms.shape[0], terms.shape[1] // 27
    cube_form = terms.reshape(batch_size, channels, 27, SIDE, SIDE, SIDE)
    padded = jnp.pad(cube_form, ((0, 0), (0, 0), (0, 0), (1, 1), (1, 1), (1, 1)))
    total = jnp.zeros((batch_size, channels, SIDE, SIDE, SIDE), jnp.float32)
    for tap_index in range(27):
        shift_depth, shift_rows, shift_cols = tap_index // 9, (tap_index // 3) % 3, tap_index % 3
        total = total + padded[:, :, tap_index, 2 - shift_depth:2 - shift_depth + SIDE, 2 - shift_rows:2 - shift_rows + SIDE, 2 - shift_cols:2 - shift_cols + SIDE]
    return total.reshape(batch_size, channels, SIDE * SIDE * SIDE)


def reference(snapshots, first_weight, second_weight, cotangent):
    first_matrix = first_weight.reshape(CH * 27, CH)
    second_matrix = second_weight.reshape(CH * 27, CH)

    def one_snapshot(carry, item):
        snapshot, grad_out = item
        input_patches = shifted(snapshot[None])[0]
        first_sum = jnp.dot(first_matrix.T, input_patches, preferred_element_type=jnp.float32)
        first_map = first_sum.astype(jnp.bfloat16)
        first_values = first_map.astype(jnp.float32)
        hidden = jax.nn.silu(first_values).astype(jnp.bfloat16)
        hidden_patches = shifted(hidden[None])[0]
        second_out = jnp.dot(second_matrix.T, hidden_patches, preferred_element_type=jnp.float32).astype(jnp.bfloat16)
        second_term = jnp.dot(hidden_patches, grad_out.T, preferred_element_type=jnp.float32)
        terms = jnp.dot(second_matrix, grad_out, preferred_element_type=jnp.float32)
        hidden_grad = spread(terms[None])[0]
        sigmoid_values = jax.nn.sigmoid(first_values)
        first_map_grad = (hidden_grad * sigmoid_values * (1.0 + first_values * (1.0 - sigmoid_values))).astype(jnp.bfloat16)
        first_term = jnp.dot(input_patches, first_map_grad.T, preferred_element_type=jnp.float32)
        return (carry[0] + first_term, carry[1] + second_term), second_out

    start_sums = (jnp.zeros((CH * 27, CH), jnp.float32), jnp.zeros((CH * 27, CH), jnp.float32))
    sums, second_out = lax.scan(one_snapshot, start_sums, (snapshots, cotangent))
    return second_out, sums[0].reshape(CH, 27, CH), sums[1].reshape(CH, 27, CH)
```

```python
import functools

import jax
import jax.numpy as jnp
from jax import lax
from jax.experimental import pallas as pl
from jax.experimental.pallas import tpu as pltpu
from jax.sharding import PartitionSpec as P

SIDE = 8
CELLS = SIDE**3
F32 = jnp.float32
BF16 = jnp.bfloat16
VMEM = pl.BlockSpec(memory_space=pltpu.VMEM)
TAPS = [(a, b, e) for a in (-1, 0, 1) for b in (-1, 0, 1) for e in (-1, 0, 1)]


def coords():
    cell = lax.broadcasted_iota(jnp.int32, (1, CELLS), 1)
    return cell >> 6, (cell >> 3) & 7, cell & 7


def moved(v, step):
    delta = 64 * step[0] + 8 * step[1] + step[2]
    if delta == 0:
        return v
    out = pltpu.roll(v, (-delta) % CELLS, 1)
    ok = None
    for at, by in zip(coords(), step):
        if by:
            good = at < SIDE - by if by > 0 else at >= -by
            ok = good if ok is None else ok & good
    return jnp.where(ok, out, 0)


def conv_part(w_ref, v, patches):
    rows = v.shape[0]
    v = v.astype(F32)
    for t, step in enumerate(TAPS):
        patches[t * rows : (t + 1) * rows, :] = moved(v, step).astype(BF16)
    return lax.dot_general(
        w_ref[...].reshape(-1, w_ref.shape[2]),
        patches[...],
        (((0,), (0,)), ((), ())),
        preferred_element_type=F32,
    )


def conv_kernel(w_ref, v_ref, o_ref, patches):
    o_ref[...] = conv_part(w_ref, v_ref[...], patches).astype(BF16)


def conv(w, v):
    taps, rows, outs = w.shape
    return pl.pallas_call(
        conv_kernel,
        out_shape=jax.ShapeDtypeStruct((outs, CELLS), BF16),
        in_specs=[VMEM] * 2,
        out_specs=VMEM,
        scratch_shapes=[pltpu.VMEM((taps * rows, CELLS), BF16)],
        name="conv",
    )(w, v)


def spread_kernel(w_ref, g_ref, o_ref):
    taps, rows, outs = w_ref.shape
    total = jnp.zeros((rows, CELLS), F32)
    for t, step in enumerate(TAPS):
        term = jnp.dot(w_ref[t], g_ref[...], preferred_element_type=F32)
        total = total + moved(term, tuple(-s for s in step))
    o_ref[...] = total


def spread(w, g):
    taps, rows, outs = w.shape
    return pl.pallas_call(
        spread_kernel,
        out_shape=jax.ShapeDtypeStruct((rows, CELLS), F32),
        in_specs=[VMEM] * 2,
        out_specs=VMEM,
        name="spread",
    )(w, g)


def grad_kernel(x_ref, g_ref, o_ref, left, right, acc):
    n = pl.program_id(0)
    ins, outs = x_ref.shape[1], g_ref.shape[1]

    @pl.when(n == 0)
    def _():
        acc[...] = jnp.zeros_like(acc)

    x = x_ref[0].astype(F32)
    g = g_ref[0].astype(F32)
    for e in range(3):
        right[e * ins : (e + 1) * ins, :] = moved(x, (0, 0, e - 1)).astype(BF16)
    for a in range(3):
        for b in range(3):
            at = (a * 3 + b) * outs
            left[at : at + outs, :] = moved(g, (1 - a, 1 - b, 0)).astype(BF16)
    acc[...] += lax.dot_general(
        left[...], right[...], (((1,), (1,)), ((), ())), preferred_element_type=F32
    )

    @pl.when(n == pl.num_programs(0) - 1)
    def _():
        for ab in range(9):
            for e in range(3):
                o_ref[ab * 3 + e] = acc[ab * outs : (ab + 1) * outs, e * ins : (e + 1) * ins]


def grad(x, g):
    count, ins, _ = x.shape
    outs = g.shape[1]
    return pl.pallas_call(
        grad_kernel,
        grid=(count,),
        out_shape=jax.ShapeDtypeStruct((27, outs, ins), F32),
        in_specs=[
            pl.BlockSpec((1, ins, CELLS), lambda n: (n, 0, 0)),
            pl.BlockSpec((1, outs, CELLS), lambda n: (n, 0, 0)),
        ],
        out_specs=pl.BlockSpec((27, outs, ins), lambda n: (0, 0, 0)),
        scratch_shapes=[
            pltpu.VMEM((9 * outs, CELLS), BF16),
            pltpu.VMEM((3 * ins, CELLS), BF16),
            pltpu.VMEM((9 * outs, 3 * ins), F32),
        ],
        name="grad",
    )(x, g)


def swap(v, axis):
    return lax.all_to_all(v, axis, 0, 0, tiled=True)


def body(samples, chans, snapshots, first_weight, second_weight, cotangent):
    ins = first_weight.shape[0]
    full = snapshots.shape[1]
    outs = full // samples
    first_w = first_weight.transpose(1, 0, 2)
    second_w = second_weight.transpose(1, 0, 2)

    part = snapshots[0].reshape(chans, ins, -1)
    packed = jnp.concatenate(
        [part, jnp.broadcast_to(cotangent, (chans,) + cotangent.shape[1:])], axis=2
    )
    packed = swap(packed, "chan")
    x = packed[:, :, : part.shape[2]].transpose(1, 0, 2).reshape(ins, CELLS)
    full_cot = packed[:, :, part.shape[2] :].reshape(full, CELLS)

    packed = jnp.concatenate(
        [jnp.broadcast_to(x, (samples,) + x.shape), full_cot.reshape(samples, outs, CELLS)], axis=1
    )
    packed = swap(packed, "sample")
    all_x, all_cot = packed[:, :ins], packed[:, ins:]

    first_parts = swap(conv(first_w, x).reshape(chans, ins, CELLS), "chan")
    hidden_grad = spread(second_w, full_cot)
    first_map = jnp.sum(first_parts.astype(F32), axis=0).astype(BF16).astype(F32)
    gate = jax.nn.sigmoid(first_map)
    hidden = (first_map * gate).astype(BF16)
    map_grad = (hidden_grad * gate * (1.0 + first_map * (1.0 - gate))).astype(BF16)

    second_parts = conv(second_w, hidden).reshape(chans, ins, CELLS)
    packed = jnp.concatenate(
        [second_parts, jnp.broadcast_to(map_grad, (chans,) + map_grad.shape)], axis=1
    )
    packed = swap(packed, "chan")
    second_out = jnp.sum(packed[:, :ins].astype(F32), axis=0).astype(BF16)
    full_map_grad = packed[:, ins:].reshape(samples, outs, CELLS)

    packed = jnp.concatenate(
        [jnp.broadcast_to(hidden, (samples,) + hidden.shape), full_map_grad], axis=1
    )
    packed = swap(packed, "sample")
    all_hidden, all_map_grad = packed[:, :ins], packed[:, ins:]

    second_grad = grad(all_hidden, all_cot)
    first_grad = grad(all_x, all_map_grad)
    return (
        second_out[None],
        first_grad.transpose(2, 0, 1),
        second_grad.transpose(2, 0, 1),
    )


def solution(mesh):
    placed = (
        P("sample", None, "chan"),
        P("chan", None, None),
        P("chan", None, None),
        P("sample", "chan", None),
    )
    return jax.shard_map(
        functools.partial(body, mesh.shape["sample"], mesh.shape["chan"]),
        mesh=mesh,
        in_specs=placed,
        out_specs=(P("sample", "chan", None), P("chan", None, "sample"), P("chan", None, "sample")),
        check_vma=False,
    )
```

```python
import functools

import jax
import jax.numpy as jnp
from jax import lax
from jax.experimental import pallas as pl
from jax.experimental.pallas import tpu as pltpu
from jax.sharding import PartitionSpec as P

SIDE = 8
CELLS = SIDE**3
F32 = jnp.float32
BF16 = jnp.bfloat16
VMEM = pl.BlockSpec(memory_space=pltpu.VMEM)
TAPS = [(a, b, e) for a in (-1, 0, 1) for b in (-1, 0, 1) for e in (-1, 0, 1)]


def coords():
    cell = lax.broadcasted_iota(jnp.int32, (1, CELLS), 1)
    return cell >> 6, (cell >> 3) & 7, cell & 7


def moved(v, step):
    delta = 64 * step[0] + 8 * step[1] + step[2]
    if delta == 0:
        return v
    out = pltpu.roll(v, (-delta) % CELLS, 1)
    ok = None
    for at, by in zip(coords(), step):
        if by:
            good = at < SIDE - by if by > 0 else at >= -by
            ok = good if ok is None else ok & good
    return jnp.where(ok, out, jnp.zeros_like(out))


def call(kernel, outs, args, scratch=(), name=None):
    return pl.pallas_call(
        kernel,
        out_shape=[jax.ShapeDtypeStruct(shape, dtype) for shape, dtype in outs],
        in_specs=[VMEM] * len(args),
        out_specs=[VMEM] * len(outs),
        scratch_shapes=list(scratch),
        name=name,
    )(*args)


def block(j, chans, width):
    start = lax.rem(lax.axis_index("chan") + j, chans) * width
    return pl.ds(pl.multiple_of(start, width), width)


def split_kernel(chans, v_ref, *outs):
    rows = outs[0].shape[0]
    for j in range(chans):
        outs[j][...] = v_ref[block(j, chans, rows), :]


def conv_part(chans, w_ref, v, outs, patches, sums):
    rows = v.shape[0]
    for t, step in enumerate(TAPS):
        patches[t * rows : (t + 1) * rows, :] = moved(v, step)
    sums[...] = lax.dot_general(
        w_ref[...].reshape(-1, w_ref.shape[2]),
        patches[...],
        (((0,), (0,)), ((), ())),
        preferred_element_type=F32,
    ).astype(BF16)
    for j in range(chans):
        outs[j][...] = sums[block(j, chans, outs[j].shape[0]), :]


def first_kernel(chans, w_ref, *refs):
    parts, (x_ref, *outs), (patches, sums) = refs[:chans], refs[chans:-2], refs[-2:]
    width = CELLS // chans
    for j in range(chans):
        x_ref[:, block(chans - j, chans, width)] = parts[j][...]
    conv_part(chans, w_ref, x_ref[...], outs, patches, sums)


def second_kernel(chans, w_ref, v_ref, *refs):
    conv_part(chans, w_ref, v_ref[...], refs[:chans], *refs[chans:])


def join_kernel(chans, *refs):
    parts, out = refs[:chans], refs[chans]
    rows = parts[0].shape[0]
    for j in range(chans):
        out[block(chans - j, chans, rows), :] = parts[j][...]


def pack_kernel(chans, x_ref, *refs):
    parts, (full, out) = refs[:chans], refs[chans:]
    join_kernel(chans, *parts, full)
    rows = x_ref.shape[0]
    outs = out.shape[1] - rows
    for s in range(out.shape[0]):
        out[s, :rows, :] = x_ref[...]
        out[s, rows:, :] = full[s * outs : (s + 1) * outs, :]


def spread_kernel(w_ref, g_ref, o_ref):
    taps, rows, outs = w_ref.shape
    total = jnp.zeros((rows, CELLS), F32)
    for t, step in enumerate(TAPS):
        term = jnp.dot(w_ref[t], g_ref[...], preferred_element_type=F32)
        total = total + moved(term, tuple(-s for s in step))
    o_ref[...] = total


def middle_kernel(chans, hidden_grad, *refs):
    parts, (hidden_ref, copies_ref, map_grad_ref) = refs[:chans], refs[chans:]
    total = parts[0][...].astype(F32)
    for j in range(1, chans):
        total = total + parts[j][...].astype(F32)
    first_map = total.astype(BF16).astype(F32)
    gate = 1.0 / (1.0 + jnp.exp(-first_map))
    hidden = (first_map * gate).astype(BF16)
    hidden_ref[...] = hidden
    for s in range(copies_ref.shape[0]):
        copies_ref[s] = hidden
    map_grad_ref[...] = (hidden_grad[...] * gate * (1.0 + first_map * (1.0 - gate))).astype(BF16)


def grad_kernel(at, x_ref, g_ref, o_ref, left, right):
    count, outs, _ = g_ref.shape
    ins = o_ref.shape[2]
    for n in range(count):
        cells = pl.ds(n * CELLS, CELLS)
        x = x_ref[n, :ins, :]
        for e in range(3):
            right[e * ins : (e + 1) * ins, cells] = moved(x, (0, 0, e - 1))
        g = g_ref[n, at:, :]
        rows = g.shape[0]
        for a in range(3):
            for b in range(3):
                row = (a * 3 + b) * rows
                left[row : row + rows, cells] = moved(g, (1 - a, 1 - b, 0))
    acc = lax.dot_general(
        left[...], right[...], (((1,), (1,)), ((), ())), preferred_element_type=F32
    )
    rows = o_ref.shape[1]
    for ab in range(9):
        for e in range(3):
            o_ref[ab * 3 + e] = acc[ab * rows : (ab + 1) * rows, e * ins : (e + 1) * ins]


def grad(x, g, ins, at):
    count = x.shape[0]
    outs = g.shape[1] - at
    return call(
        functools.partial(grad_kernel, at),
        [((27, outs, ins), F32)],
        [x, g],
        [
            pltpu.VMEM((9 * outs, count * CELLS), BF16),
            pltpu.VMEM((3 * ins, count * CELLS), BF16),
        ],
        name="grad",
    )[0]


def swap(v, axis):
    return lax.all_to_all(v, axis, 0, 0, tiled=True)


def send(v, step, size):
    return lax.ppermute(v, "chan", [(k, (k + step) % size) for k in range(size)])


def exchange(parts, size):
    return [parts[0]] + [send(parts[j], j, size) for j in range(1, size)]


def body(samples, chans, snapshots, first_weight, second_weight, cotangent):
    ins = first_weight.shape[0]
    full = snapshots.shape[1]
    outs = full // samples
    width = CELLS // chans
    run = lambda kernel: functools.partial(kernel, chans)
    first_w = first_weight.transpose(1, 0, 2)
    second_w = second_weight.transpose(1, 0, 2)
    patches = [pltpu.VMEM((27 * ins, CELLS), BF16), pltpu.VMEM((full, CELLS), BF16)]
    piece = ((ins, CELLS), BF16)

    cots = exchange([cotangent[0]] * chans, chans)
    if width % 128 == 0:
        cells = [((ins, width), BF16)] * chans
        cells = exchange(call(run(split_kernel), cells, [snapshots[0]], name="split"), chans)
        x, *parts = call(
            run(first_kernel), [piece] * (chans + 1), [first_w] + cells, patches, "first"
        )
    else:
        x = swap(snapshots[0].reshape(chans, ins, width), "chan")
        x = x.transpose(1, 0, 2).reshape(ins, CELLS)
        parts = call(run(second_kernel), [piece] * chans, [first_w, x], patches, "first")
    parts = exchange(parts, chans)
    full_cot, packed = call(
        run(pack_kernel),
        [((full, CELLS), BF16), ((samples, ins + outs, CELLS), BF16)],
        [x] + cots,
        name="pack",
    )
    packed = swap(packed, "sample")
    hidden_grad = call(spread_kernel, [((ins, CELLS), F32)], [second_w, full_cot], name="spread")[0]
    hidden, copies, map_grad = call(
        run(middle_kernel),
        [piece, ((samples, ins, CELLS), BF16), piece],
        [hidden_grad] + parts,
        name="middle",
    )
    all_hidden = swap(copies, "sample")
    map_grads = exchange([map_grad] * chans, chans)
    parts = exchange(
        call(run(second_kernel), [piece] * chans, [second_w, hidden], patches, "second"), chans
    )
    full_map_grad = call(run(join_kernel), [((full, CELLS), BF16)], map_grads, name="join")[0]
    all_map_grad = swap(full_map_grad.reshape(samples, outs, CELLS), "sample")
    second_out = sum(p.astype(F32) for p in parts).astype(BF16)
    second_grad = grad(all_hidden, packed, ins, ins)
    first_grad = grad(packed, all_map_grad, ins, 0)
    return (
        second_out[None],
        first_grad.transpose(2, 0, 1),
        second_grad.transpose(2, 0, 1),
    )


def solution(mesh):
    placed = (
        P("sample", None, "chan"),
        P("chan", None, None),
        P("chan", None, None),
        P("sample", "chan", None),
    )
    return jax.shard_map(
        functools.partial(body, mesh.shape["sample"], mesh.shape["chan"]),
        mesh=mesh,
        in_specs=placed,
        out_specs=(P("sample", "chan", None), P("chan", None, "sample"), P("chan", None, "sample")),
        check_vma=False,
    )
```

```python
import functools

import jax
import jax.numpy as jnp
from jax import lax
from jax.experimental import pallas as pl
from jax.experimental.pallas import tpu as pltpu
from jax.sharding import PartitionSpec as P

SIDE = 8
CELLS = SIDE**3
F32 = jnp.float32
BF16 = jnp.bfloat16
VMEM = pl.BlockSpec(memory_space=pltpu.VMEM)
TAPS = [(a, b, e) for a in (-1, 0, 1) for b in (-1, 0, 1) for e in (-1, 0, 1)]


def coords():
    cell = lax.broadcasted_iota(jnp.int32, (1, CELLS), 1)
    return cell >> 6, (cell >> 3) & 7, cell & 7


def moved(v, step):
    delta = 64 * step[0] + 8 * step[1] + step[2]
    if delta == 0:
        return v
    out = pltpu.roll(v, (-delta) % CELLS, 1)
    ok = None
    for at, by in zip(coords(), step):
        if by:
            good = at < SIDE - by if by > 0 else at >= -by
            ok = good if ok is None else ok & good
    return jnp.where(ok, out, jnp.zeros_like(out))


def call(kernel, outs, args, scratch=(), name=None, us=1.0):
    return pl.pallas_call(
        kernel,
        out_shape=[jax.ShapeDtypeStruct(shape, dtype) for shape, dtype in outs],
        in_specs=[VMEM] * len(args),
        out_specs=[VMEM] * len(outs),
        scratch_shapes=list(scratch),
        cost_estimate=pl.CostEstimate(
            flops=int(us * 1.1e9), bytes_accessed=int(us * 3.0e6), transcendentals=0
        ),
        name=name,
    )(*args)


def block(j, chans, width):
    start = lax.rem(lax.axis_index("chan") + j, chans) * width
    return pl.ds(pl.multiple_of(start, width), width)


def split_kernel(chans, v_ref, g_ref, own, *outs):
    rows, width = own.shape
    own[...] = v_ref[block(0, chans, rows), :]
    for j, out in enumerate(outs):
        out[:, :width] = v_ref[block(j + 1, chans, rows), :]
        out[:, width:] = g_ref[...]


def conv_part(chans, w_ref, v, outs, patches, sums):
    rows = v.shape[0]
    for t, step in enumerate(TAPS):
        patches[t * rows : (t + 1) * rows, :] = moved(v, step)
    sums[...] = lax.dot_general(
        w_ref[...].reshape(-1, w_ref.shape[2]),
        patches[...],
        (((0,), (0,)), ((), ())),
        preferred_element_type=F32,
    ).astype(BF16)
    for j in range(chans):
        outs[j][...] = sums[block(j, chans, outs[j].shape[0]), :]


def first_kernel(chans, w_ref, own, g_ref, *refs):
    parts, (packed, full, *outs), scratch = refs[: chans - 1], refs[chans - 1 : -3], refs[-3:]
    x, *scratch = scratch
    rows, width = own.shape
    x[:, block(0, chans, width)] = own[...]
    full[block(0, chans, rows), :] = g_ref[...]
    for j, part in enumerate(parts):
        x[:, block(chans - j - 1, chans, width)] = part[:, :width]
        full[block(chans - j - 1, chans, rows), :] = part[:, width:]
    conv_part(chans, w_ref, x[...], outs, *scratch)
    fill(packed, x, full)


def fill(packed, x, full):
    rows = x.shape[0]
    outs = packed.shape[1] - rows
    for s in range(packed.shape[0]):
        packed[s, :rows, :] = x[...]
        packed[s, rows:, :] = full[s * outs : (s + 1) * outs, :]


def second_kernel(chans, w_ref, v_ref, *refs):
    conv_part(chans, w_ref, v_ref[...], refs[:chans], *refs[chans:])


def join_kernel(chans, *refs):
    parts, out = refs[:chans], refs[chans]
    rows = parts[0].shape[0]
    for j in range(chans):
        out[block(chans - j, chans, rows), :] = parts[j][...]


def pack_kernel(chans, x_ref, *refs):
    parts, (packed, full) = refs[:chans], refs[chans:]
    join_kernel(chans, *parts, full)
    fill(packed, x_ref, full)


def spread_kernel(w_ref, g_ref, o_ref):
    taps, rows, outs = w_ref.shape
    total = jnp.zeros((rows, CELLS), F32)
    for t, step in enumerate(TAPS):
        term = jnp.dot(w_ref[t], g_ref[...], preferred_element_type=F32)
        total = total + moved(term, tuple(-s for s in step))
    o_ref[...] = total


def middle_kernel(chans, hidden_grad, *refs):
    parts, (hidden_ref, copies_ref, map_grad_ref) = refs[:chans], refs[chans:]
    total = parts[0][...].astype(F32)
    for j in range(1, chans):
        total = total + parts[j][...].astype(F32)
    first_map = total.astype(BF16).astype(F32)
    gate = 1.0 / (1.0 + jnp.exp(-first_map))
    hidden = (first_map * gate).astype(BF16)
    hidden_ref[...] = hidden
    for s in range(copies_ref.shape[0]):
        copies_ref[s] = hidden
    map_grad_ref[...] = (hidden_grad[...] * gate * (1.0 + first_map * (1.0 - gate))).astype(BF16)


def grad_kernel(at, x_ref, g_ref, o_ref, left, right):
    count, outs, _ = g_ref.shape
    ins = o_ref.shape[2]
    for n in range(count):
        cells = pl.ds(n * CELLS, CELLS)
        x = x_ref[n, :ins, :]
        for e in range(3):
            right[e * ins : (e + 1) * ins, cells] = moved(x, (0, 0, e - 1))
        g = g_ref[n, at:, :]
        rows = g.shape[0]
        for a in range(3):
            for b in range(3):
                row = (a * 3 + b) * rows
                left[row : row + rows, cells] = moved(g, (1 - a, 1 - b, 0))
    acc = lax.dot_general(
        left[...], right[...], (((1,), (1,)), ((), ())), preferred_element_type=F32
    )
    rows = o_ref.shape[1]
    for ab in range(9):
        for e in range(3):
            o_ref[ab * 3 + e] = acc[ab * rows : (ab + 1) * rows, e * ins : (e + 1) * ins]


def grad(x, g, ins, at):
    count = x.shape[0]
    outs = g.shape[1] - at
    return call(
        functools.partial(grad_kernel, at),
        [((27, outs, ins), F32)],
        [x, g],
        [
            pltpu.VMEM((9 * outs, count * CELLS), BF16),
            pltpu.VMEM((3 * ins, count * CELLS), BF16),
        ],
        name="grad",
        us=3.0,
    )[0]


def swap(v, axis):
    return lax.all_to_all(v, axis, 0, 0, tiled=True)


def send(v, step, size):
    return lax.ppermute(v, "chan", [(k, (k + step) % size) for k in range(size)])


def exchange(parts, size):
    return [parts[0]] + [send(parts[j], j, size) for j in range(1, size)]


def body(samples, chans, snapshots, first_weight, second_weight, cotangent):
    ins = first_weight.shape[0]
    full = snapshots.shape[1]
    outs = full // samples
    width = CELLS // chans
    run = lambda kernel: functools.partial(kernel, chans)
    first_w = first_weight.transpose(1, 0, 2)
    second_w = second_weight.transpose(1, 0, 2)
    patches = [pltpu.VMEM((27 * ins, CELLS), BF16), pltpu.VMEM((full, CELLS), BF16)]
    piece = ((ins, CELLS), BF16)

    gathered = [((samples, ins + outs, CELLS), BF16), ((full, CELLS), BF16)]
    if width % 128 == 0:
        cells = [((ins, width), BF16)] + [((ins, width + CELLS), BF16)] * (chans - 1)
        cells = call(run(split_kernel), cells, [snapshots[0], cotangent[0]], name="split")
        own, *cells = exchange(cells, chans)
        packed, full_cot, *parts = call(
            run(first_kernel),
            gathered + [piece] * chans,
            [first_w, own, cotangent[0]] + cells,
            [pltpu.VMEM((ins, CELLS), BF16)] + patches,
            "first",
            3.0,
        )
    else:
        x = swap(snapshots[0].reshape(chans, ins, width), "chan")
        x = x.transpose(1, 0, 2).reshape(ins, CELLS)
        parts = call(run(second_kernel), [piece] * chans, [first_w, x], patches, "first", 2.8)
        cots = exchange([cotangent[0]] * chans, chans)
        packed, full_cot = call(run(pack_kernel), gathered, [x] + cots, name="pack")
    parts = exchange(parts, chans)
    packed = swap(packed, "sample")
    hidden_grad = call(spread_kernel, [((ins, CELLS), F32)], [second_w, full_cot], (), "spread", 3.4)[0]
    hidden, copies, map_grad = call(
        run(middle_kernel),
        [piece, ((samples, ins, CELLS), BF16), piece],
        [hidden_grad] + parts,
        name="middle",
        us=2.0,
    )
    copies, packed = lax.optimization_barrier((copies, packed))
    all_hidden = swap(copies, "sample")
    map_grads = exchange([map_grad] * chans, chans)
    parts = exchange(
        call(run(second_kernel), [piece] * chans, [second_w, hidden], patches, "second", 2.8), chans
    )
    full_map_grad = call(run(join_kernel), [((full, CELLS), BF16)], map_grads, name="join")[0]
    full_map_grad, all_hidden = lax.optimization_barrier((full_map_grad, all_hidden))
    all_map_grad = swap(full_map_grad.reshape(samples, outs, CELLS), "sample")
    second_out = sum(p.astype(F32) for p in parts).astype(BF16)
    second_grad = grad(all_hidden, packed, ins, ins)
    first_grad = grad(packed, all_map_grad, ins, 0)
    return (
        second_out[None],
        first_grad.transpose(2, 0, 1),
        second_grad.transpose(2, 0, 1),
    )


def solution(mesh):
    placed = (
        P("sample", None, "chan"),
        P("chan", None, None),
        P("chan", None, None),
        P("sample", "chan", None),
    )
    return jax.shard_map(
        functools.partial(body, mesh.shape["sample"], mesh.shape["chan"]),
        mesh=mesh,
        in_specs=placed,
        out_specs=(P("sample", "chan", None), P("chan", None, "sample"), P("chan", None, "sample")),
        check_vma=False,
    )
```

```python
import functools

import jax
import jax.numpy as jnp
from jax import lax
from jax.experimental import pallas as pl
from jax.experimental.pallas import tpu as pltpu
from jax.sharding import PartitionSpec as P

SIDE = 8
CELLS = SIDE**3
F32 = jnp.float32
BF16 = jnp.bfloat16
VMEM = pl.BlockSpec(memory_space=pltpu.VMEM)
TAPS = [(a, b, e) for a in (-1, 0, 1) for b in (-1, 0, 1) for e in (-1, 0, 1)]


def coords():
    cell = lax.broadcasted_iota(jnp.int32, (1, CELLS), 1)
    return cell >> 6, (cell >> 3) & 7, cell & 7


def moved(v, step):
    delta = 64 * step[0] + 8 * step[1] + step[2]
    if delta == 0:
        return v
    out = pltpu.roll(v, (-delta) % CELLS, 1)
    ok = None
    for at, by in zip(coords(), step):
        if by:
            good = at < SIDE - by if by > 0 else at >= -by
            ok = good if ok is None else ok & good
    return jnp.where(ok, out, jnp.zeros_like(out))


def call(kernel, outs, args, scratch=(), name=None, us=1.0):
    return pl.pallas_call(
        kernel,
        out_shape=[jax.ShapeDtypeStruct(shape, dtype) for shape, dtype in outs],
        in_specs=[VMEM] * len(args),
        out_specs=[VMEM] * len(outs),
        scratch_shapes=list(scratch),
        cost_estimate=pl.CostEstimate(
            flops=int(us * 1.1e9), bytes_accessed=int(us * 3.0e6), transcendentals=0
        ),
        compiler_params=pltpu.CompilerParams(vmem_limit_bytes=16 << 20),
        name=name,
    )(*args)


def block(j, chans, width):
    start = lax.rem(lax.axis_index("chan") + j, chans) * width
    return pl.ds(pl.multiple_of(start, width), width)


def split_kernel(chans, v_ref, g_ref, own, *outs):
    rows, width = own.shape
    own[...] = v_ref[block(0, chans, rows), :]
    for j, out in enumerate(outs):
        out[:, :width] = v_ref[block(j + 1, chans, rows), :]
        out[:, width:] = g_ref[...]


def conv_part(chans, w_ref, v, outs, patches, sums):
    rows = v.shape[0]
    for t, step in enumerate(TAPS):
        patches[t * rows : (t + 1) * rows, :] = moved(v, step)
    sums[...] = lax.dot_general(
        w_ref[...].reshape(-1, w_ref.shape[2]),
        patches[...],
        (((0,), (0,)), ((), ())),
        preferred_element_type=F32,
    ).astype(BF16)
    for j in range(chans):
        outs[j][...] = sums[block(j, chans, outs[j].shape[0]), :]


def first_kernel(chans, w_ref, own, g_ref, *refs):
    parts, (packed, full, *outs), scratch = refs[: chans - 1], refs[chans - 1 : -3], refs[-3:]
    x, *scratch = scratch
    rows, width = own.shape
    x[:, block(0, chans, width)] = own[...]
    full[block(0, chans, rows), :] = g_ref[...]
    for j, part in enumerate(parts):
        x[:, block(chans - j - 1, chans, width)] = part[:, :width]
        full[block(chans - j - 1, chans, rows), :] = part[:, width:]
    conv_part(chans, w_ref, x[...], outs, *scratch)
    fill(packed, x, full)


def fill(packed, x, full):
    rows = x.shape[0]
    outs = packed.shape[1] - rows
    for s in range(packed.shape[0]):
        packed[s, :rows, :] = x[...]
        packed[s, rows:, :] = full[s * outs : (s + 1) * outs, :]


def second_kernel(chans, w_ref, v_ref, *refs):
    conv_part(chans, w_ref, v_ref[...], refs[:chans], *refs[chans:])


def join_kernel(chans, *refs):
    parts, out = refs[:chans], refs[chans]
    rows = parts[0].shape[0]
    for j in range(chans):
        out[block(chans - j, chans, rows), :] = parts[j][...]


def pack_kernel(chans, x_ref, *refs):
    parts, (packed, full) = refs[:chans], refs[chans:]
    join_kernel(chans, *parts, full)
    fill(packed, x_ref, full)


def spread_kernel(w_ref, g_ref, o_ref):
    taps, rows, outs = w_ref.shape
    total = jnp.zeros((rows, CELLS), F32)
    for t, step in enumerate(TAPS):
        term = jnp.dot(w_ref[t], g_ref[...], preferred_element_type=F32)
        total = total + moved(term, tuple(-s for s in step))
    o_ref[...] = total


def middle_kernel(chans, hidden_grad, *refs):
    parts, (hidden_ref, copies_ref, map_grad_ref) = refs[:chans], refs[chans:]
    total = parts[0][...].astype(F32)
    for j in range(1, chans):
        total = total + parts[j][...].astype(F32)
    first_map = total.astype(BF16).astype(F32)
    gate = 1.0 / (1.0 + jnp.exp(-first_map))
    hidden = (first_map * gate).astype(BF16)
    hidden_ref[...] = hidden
    for s in range(copies_ref.shape[0]):
        copies_ref[s] = hidden
    map_grad_ref[...] = (hidden_grad[...] * gate * (1.0 + first_map * (1.0 - gate))).astype(BF16)


def grad_kernel(at, x_ref, g_ref, o_ref, left, right):
    count, outs, _ = g_ref.shape
    ins = o_ref.shape[2]
    for n in range(count):
        cells = pl.ds(n * CELLS, CELLS)
        x = x_ref[n, :ins, :]
        for e in range(3):
            right[e * ins : (e + 1) * ins, cells] = moved(x, (0, 0, e - 1))
        g = g_ref[n, at:, :]
        rows = g.shape[0]
        for a in range(3):
            for b in range(3):
                row = (a * 3 + b) * rows
                left[row : row + rows, cells] = moved(g, (1 - a, 1 - b, 0))
    acc = lax.dot_general(
        left[...], right[...], (((1,), (1,)), ((), ())), preferred_element_type=F32
    )
    rows = o_ref.shape[1]
    for ab in range(9):
        for e in range(3):
            o_ref[ab * 3 + e] = acc[ab * rows : (ab + 1) * rows, e * ins : (e + 1) * ins]


def grad(x, g, ins, at):
    count = x.shape[0]
    outs = g.shape[1] - at
    return call(
        functools.partial(grad_kernel, at),
        [((27, outs, ins), F32)],
        [x, g],
        [
            pltpu.VMEM((9 * outs, count * CELLS), BF16),
            pltpu.VMEM((3 * ins, count * CELLS), BF16),
        ],
        name="grad",
        us=3.0,
    )[0]


def swap(v, axis):
    return lax.all_to_all(v, axis, 0, 0, tiled=True)


def send(v, step, size):
    return lax.ppermute(v, "chan", [(k, (k + step) % size) for k in range(size)])


def exchange(parts, size):
    return [parts[0]] + [send(parts[j], j, size) for j in range(1, size)]


def body(samples, chans, snapshots, first_weight, second_weight, cotangent):
    ins = first_weight.shape[0]
    full = snapshots.shape[1]
    outs = full // samples
    width = CELLS // chans
    run = lambda kernel: functools.partial(kernel, chans)
    first_w = first_weight.transpose(1, 0, 2)
    second_w = second_weight.transpose(1, 0, 2)
    patches = [pltpu.VMEM((27 * ins, CELLS), BF16), pltpu.VMEM((full, CELLS), BF16)]
    piece = ((ins, CELLS), BF16)

    gathered = [((samples, ins + outs, CELLS), BF16), ((full, CELLS), BF16)]
    if width % 128 == 0:
        cells = [((ins, width), BF16)] + [((ins, width + CELLS), BF16)] * (chans - 1)
        cells = call(run(split_kernel), cells, [snapshots[0], cotangent[0]], name="split")
        own, *cells = exchange(cells, chans)
        packed, full_cot, *parts = call(
            run(first_kernel),
            gathered + [piece] * chans,
            [first_w, own, cotangent[0]] + cells,
            [pltpu.VMEM((ins, CELLS), BF16)] + patches,
            "first",
            3.0,
        )
    else:
        x = swap(snapshots[0].reshape(chans, ins, width), "chan")
        x = x.transpose(1, 0, 2).reshape(ins, CELLS)
        parts = call(run(second_kernel), [piece] * chans, [first_w, x], patches, "first", 2.8)
        cots = exchange([cotangent[0]] * chans, chans)
        packed, full_cot = call(run(pack_kernel), gathered, [x] + cots, name="pack")
    parts = exchange(parts, chans)
    packed = swap(packed, "sample")
    hidden_grad = call(spread_kernel, [((ins, CELLS), F32)], [second_w, full_cot], (), "spread", 3.4)[0]
    hidden, copies, map_grad = call(
        run(middle_kernel),
        [piece, ((samples, ins, CELLS), BF16), piece],
        [hidden_grad] + parts,
        name="middle",
        us=2.0,
    )
    copies, packed = lax.optimization_barrier((copies, packed))
    all_hidden = swap(copies, "sample")
    map_grads = exchange([map_grad] * chans, chans)
    parts = exchange(
        call(run(second_kernel), [piece] * chans, [second_w, hidden], patches, "second", 2.8), chans
    )
    full_map_grad = call(run(join_kernel), [((full, CELLS), BF16)], map_grads, name="join")[0]
    full_map_grad, all_hidden = lax.optimization_barrier((full_map_grad, all_hidden))
    all_map_grad = swap(full_map_grad.reshape(samples, outs, CELLS), "sample")
    second_out = sum(p.astype(F32) for p in parts).astype(BF16)
    second_grad = grad(all_hidden, packed, ins, ins)
    first_grad = grad(packed, all_map_grad, ins, 0)
    return (
        second_out[None],
        first_grad.transpose(2, 0, 1),
        second_grad.transpose(2, 0, 1),
    )


def solution(mesh):
    placed = (
        P("sample", None, "chan"),
        P("chan", None, None),
        P("chan", None, None),
        P("sample", "chan", None),
    )
    return jax.shard_map(
        functools.partial(body, mesh.shape["sample"], mesh.shape["chan"]),
        mesh=mesh,
        in_specs=placed,
        out_specs=(P("sample", "chan", None), P("chan", None, "sample"), P("chan", None, "sample")),
        check_vma=False,
    )
```

```python
import functools

import jax
import jax.numpy as jnp
from jax import lax
from jax.experimental import pallas as pl
from jax.experimental.pallas import tpu as pltpu
from jax.sharding import PartitionSpec as P

SIDE = 8
CELLS = SIDE**3
F32 = jnp.float32
BF16 = jnp.bfloat16
VMEM = pl.BlockSpec(memory_space=pltpu.VMEM)
TAPS = [(a, b, e) for a in (-1, 0, 1) for b in (-1, 0, 1) for e in (-1, 0, 1)]


def coords():
    cell = lax.broadcasted_iota(jnp.int32, (1, CELLS), 1)
    return cell >> 6, (cell >> 3) & 7, cell & 7


def moved(v, step):
    delta = 64 * step[0] + 8 * step[1] + step[2]
    if delta == 0:
        return v
    out = pltpu.roll(v, (-delta) % CELLS, 1)
    ok = None
    for at, by in zip(coords(), step):
        if by:
            good = at < SIDE - by if by > 0 else at >= -by
            ok = good if ok is None else ok & good
    return jnp.where(ok, out, jnp.zeros_like(out))


def call(kernel, outs, args, scratch=(), name=None, us=1.0):
    return pl.pallas_call(
        kernel,
        out_shape=[jax.ShapeDtypeStruct(shape, dtype) for shape, dtype in outs],
        in_specs=[VMEM] * len(args),
        out_specs=[VMEM] * len(outs),
        scratch_shapes=list(scratch),
        cost_estimate=pl.CostEstimate(
            flops=int(us * 1.1e9), bytes_accessed=int(us * 3.0e6), transcendentals=0
        ),
        compiler_params=pltpu.CompilerParams(vmem_limit_bytes=16 << 20),
        name=name,
    )(*args)


def block(j, chans, width):
    start = lax.rem(lax.axis_index("chan") + j, chans) * width
    return pl.ds(pl.multiple_of(start, width), width)


def split_kernel(chans, v_ref, g_ref, own, *outs):
    rows, width = own.shape
    own[...] = v_ref[block(0, chans, rows), :]
    for j, out in enumerate(outs):
        out[:, :width] = v_ref[block(j + 1, chans, rows), :]
        out[:, width:] = g_ref[...]


def conv_part(chans, w_ref, v, outs, patches, sums):
    rows = v.shape[0]
    for t, step in enumerate(TAPS):
        patches[t * rows : (t + 1) * rows, :] = moved(v, step)
    sums[...] = lax.dot_general(
        w_ref[...].reshape(-1, w_ref.shape[2]),
        patches[...],
        (((0,), (0,)), ((), ())),
        preferred_element_type=F32,
    ).astype(BF16)
    for j in range(chans):
        outs[j][...] = sums[block(j, chans, outs[j].shape[0]), :]


def first_kernel(chans, w_ref, own, g_ref, *refs):
    parts, (packed, full, *outs), scratch = refs[: chans - 1], refs[chans - 1 : -3], refs[-3:]
    x, *scratch = scratch
    rows, width = own.shape
    x[:, block(0, chans, width)] = own[...]
    full[block(0, chans, rows), :] = g_ref[...]
    for j, part in enumerate(parts):
        x[:, block(chans - j - 1, chans, width)] = part[:, :width]
        full[block(chans - j - 1, chans, rows), :] = part[:, width:]
    conv_part(chans, w_ref, x[...], outs, *scratch)
    fill(packed, x, full)


def fill(packed, x, full):
    rows = x.shape[0]
    outs = packed.shape[1] - rows
    for s in range(packed.shape[0]):
        packed[s, :rows, :] = x[...]
        packed[s, rows:, :] = full[s * outs : (s + 1) * outs, :]


def second_kernel(chans, w_ref, v_ref, *refs):
    conv_part(chans, w_ref, v_ref[...], refs[:chans], *refs[chans:])


def join_kernel(chans, *refs):
    parts, out = refs[:chans], refs[chans]
    rows = parts[0].shape[0]
    for j in range(chans):
        out[block(chans - j, chans, rows), :] = parts[j][...]


def pack_kernel(chans, x_ref, *refs):
    parts, (packed, full) = refs[:chans], refs[chans:]
    join_kernel(chans, *parts, full)
    fill(packed, x_ref, full)


def spread_kernel(w_ref, g_ref, o_ref):
    taps, rows, outs = w_ref.shape
    total = jnp.zeros((rows, CELLS), F32)
    for t, step in enumerate(TAPS):
        term = jnp.dot(w_ref[t], g_ref[...], preferred_element_type=F32)
        total = total + moved(term, tuple(-s for s in step))
    o_ref[...] = total


def middle_kernel(chans, hidden_grad, *refs):
    parts, (hidden_ref, copies_ref, map_grad_ref) = refs[:chans], refs[chans:]
    total = parts[0][...].astype(F32)
    for j in range(1, chans):
        total = total + parts[j][...].astype(F32)
    first_map = total.astype(BF16).astype(F32)
    gate = 1.0 / (1.0 + jnp.exp(-first_map))
    hidden = (first_map * gate).astype(BF16)
    hidden_ref[...] = hidden
    for s in range(copies_ref.shape[0]):
        copies_ref[s] = hidden
    map_grad_ref[...] = (hidden_grad[...] * gate * (1.0 + first_map * (1.0 - gate))).astype(BF16)


def grad_sum(pairs, o_ref, left, right):
    for n, (x, g) in enumerate(pairs):
        cells = pl.ds(n * CELLS, CELLS)
        ins, outs = x.shape[0], g.shape[0]
        for e in range(3):
            right[e * ins : (e + 1) * ins, cells] = moved(x, (0, 0, e - 1))
        for a in range(3):
            for b in range(3):
                row = (a * 3 + b) * outs
                left[row : row + outs, cells] = moved(g, (1 - a, 1 - b, 0))
    acc = lax.dot_general(
        left[...], right[...], (((1,), (1,)), ((), ())), preferred_element_type=F32
    )
    for ab in range(9):
        for e in range(3):
            o_ref[ab * 3 + e] = acc[ab * outs : (ab + 1) * outs, e * ins : (e + 1) * ins]


def grad_kernel(at, x_ref, g_ref, o_ref, left, right):
    ins = o_ref.shape[2]
    pairs = [(x_ref[n, :ins, :], g_ref[n, at:, :]) for n in range(x_ref.shape[0])]
    grad_sum(pairs, o_ref, left, right)


def grad(x, g, ins, at):
    count = x.shape[0]
    outs = g.shape[1] - at
    return call(
        functools.partial(grad_kernel, at),
        [((27, outs, ins), F32)],
        [x, g],
        [
            pltpu.VMEM((9 * outs, count * CELLS), BF16),
            pltpu.VMEM((3 * ins, count * CELLS), BF16),
        ],
        name="grad",
        us=3.0,
    )[0]


def swap(v, axis):
    return lax.all_to_all(v, axis, 0, 0, tiled=True)


def send(v, step, size):
    return lax.ppermute(v, "chan", [(k, (k + step) % size) for k in range(size)])


def exchange(parts, size):
    return [parts[0]] + [send(parts[j], j, size) for j in range(1, size)]


def plain_body(samples, chans, snapshots, first_weight, second_weight, cotangent):
    ins = first_weight.shape[0]
    full = snapshots.shape[1]
    outs = full // samples
    width = CELLS // chans
    run = lambda kernel: functools.partial(kernel, chans)
    first_w = first_weight.transpose(1, 0, 2)
    second_w = second_weight.transpose(1, 0, 2)
    patches = [pltpu.VMEM((27 * ins, CELLS), BF16), pltpu.VMEM((full, CELLS), BF16)]
    piece = ((ins, CELLS), BF16)

    gathered = [((samples, ins + outs, CELLS), BF16), ((full, CELLS), BF16)]
    if width % 128 == 0:
        cells = [((ins, width), BF16)] + [((ins, width + CELLS), BF16)] * (chans - 1)
        cells = call(run(split_kernel), cells, [snapshots[0], cotangent[0]], name="split")
        own, *cells = exchange(cells, chans)
        packed, full_cot, *parts = call(
            run(first_kernel),
            gathered + [piece] * chans,
            [first_w, own, cotangent[0]] + cells,
            [pltpu.VMEM((ins, CELLS), BF16)] + patches,
            "first",
            3.0,
        )
    else:
        x = swap(snapshots[0].reshape(chans, ins, width), "chan")
        x = x.transpose(1, 0, 2).reshape(ins, CELLS)
        parts = call(run(second_kernel), [piece] * chans, [first_w, x], patches, "first", 2.8)
        cots = exchange([cotangent[0]] * chans, chans)
        packed, full_cot = call(run(pack_kernel), gathered, [x] + cots, name="pack")
    parts = exchange(parts, chans)
    packed = swap(packed, "sample")
    hidden_grad = call(spread_kernel, [((ins, CELLS), F32)], [second_w, full_cot], (), "spread", 3.4)[0]
    hidden, copies, map_grad = call(
        run(middle_kernel),
        [piece, ((samples, ins, CELLS), BF16), piece],
        [hidden_grad] + parts,
        name="middle",
        us=2.0,
    )
    copies, packed = lax.optimization_barrier((copies, packed))
    all_hidden = swap(copies, "sample")
    map_grads = exchange([map_grad] * chans, chans)
    parts = exchange(
        call(run(second_kernel), [piece] * chans, [second_w, hidden], patches, "second", 2.8), chans
    )
    full_map_grad = call(run(join_kernel), [((full, CELLS), BF16)], map_grads, name="join")[0]
    full_map_grad, all_hidden = lax.optimization_barrier((full_map_grad, all_hidden))
    all_map_grad = swap(full_map_grad.reshape(samples, outs, CELLS), "sample")
    second_out = sum(p.astype(F32) for p in parts).astype(BF16)
    second_grad = grad(all_hidden, packed, ins, ins)
    first_grad = grad(packed, all_map_grad, ins, 0)
    return (
        second_out[None],
        first_grad.transpose(2, 0, 1),
        second_grad.transpose(2, 0, 1),
    )


def half(rows):
    return pl.ds(pl.multiple_of((lax.axis_index("sample") & 1) * rows, rows), rows)


def far(step, rows):
    chip = (lax.axis_index("sample") >> 1) ^ step
    return pl.ds(pl.multiple_of(chip * rows, rows), rows)


def cells_kernel(chans, v_ref, *outs):
    for j, out in enumerate(outs):
        out[...] = v_ref[block(j, chans, out.shape[0]), :]


def input_kernel(chans, w_ref, *refs):
    parts, (x, *outs), scratch = refs[:chans], refs[chans:-2], refs[-2:]
    for j, part in enumerate(parts):
        x[:, block(chans - j, chans, part.shape[1])] = part[...]
    conv_part(chans, w_ref, x[...], outs, *scratch)


def pieces_kernel(hidden, x, full, out):
    rows = x.shape[0]
    for chip in range(out.shape[0]):
        out[chip, :rows, :] = hidden[...]
        out[chip, rows : 2 * rows, :] = x[...]
        out[chip, 2 * rows :, :] = full[chip * rows : (chip + 1) * rows, :]


def gate_kernel(chans, hidden_grad, *refs):
    parts, (hidden_ref, keep, give, both) = refs[:chans], refs[chans:]
    total = parts[0][...].astype(F32)
    for j in range(1, chans):
        total = total + parts[j][...].astype(F32)
    first_map = total.astype(BF16).astype(F32)
    gate = 1.0 / (1.0 + jnp.exp(-first_map))
    hidden_ref[...] = (first_map * gate).astype(BF16)
    both[...] = (hidden_grad[...] * gate * (1.0 + first_map * (1.0 - gate))).astype(BF16)
    rows = keep.shape[0]
    keep[...] = both[half(rows), :]
    other = pl.multiple_of((1 - (lax.axis_index("sample") & 1)) * rows, rows)
    give[...] = both[pl.ds(other, rows), :]


def output_kernel(chans, w_ref, v_ref, top, bottom, *refs):
    outs, scratch = refs[:chans], refs[chans:]
    rows, half_rows = v_ref.shape[0], top.shape[0]
    conv_part(chans, w_ref, v_ref[...], [out.at[:rows] for out in outs], *scratch)
    for out in outs:
        out[rows : rows + half_rows, :] = top[...]
        out[rows + half_rows :, :] = bottom[...]


def route_kernel(chans, *refs):
    parts, outs, full = refs[:chans], refs[chans:-1], refs[-1]
    rows = outs[0].shape[0]
    join_kernel(chans, *[part.at[rows:] for part in parts], full)
    for step, out in enumerate(outs):
        out[...] = full[far(step, rows), :]


def total_kernel(*refs):
    *parts, out = refs
    rows = out.shape[0]
    total = parts[0][:rows, :].astype(F32)
    for part in parts[1:]:
        total = total + part[:rows, :].astype(F32)
    out[...] = total.astype(BF16)


def second_grad_kernel(mine, other, *rest):
    rows, ins = rest[0].shape[1:]
    start = pl.multiple_of(2 * ins + (lax.axis_index("sample") & 1) * rows, rows)
    pairs = []
    for chip in range(mine.shape[0]):
        for v in (mine, other):
            pairs.append((v[chip, :ins, :], v[chip, pl.ds(start, rows), :]))
    grad_sum(pairs, *rest)


def first_grad_kernel(mine, other, *refs):
    maps, rest = refs[:-3], refs[-3:]
    rows, ins = rest[0].shape[1:]
    pairs = []
    for step, g in enumerate(maps):
        chip = (lax.axis_index("sample") >> 1) ^ step
        for core, v in enumerate((mine, other)):
            at = core * rows
            pairs.append((v[chip, ins : 2 * ins, :], g[at : at + rows, :]))
    grad_sum(pairs, *rest)


def body(samples, chans, snapshots, first_weight, second_weight, cotangent):
    ins = first_weight.shape[0]
    full = snapshots.shape[1]
    outs = full // samples
    chips = samples // 2
    run = lambda kernel: functools.partial(kernel, chans)
    first_w = first_weight.transpose(1, 0, 2)
    second_w = second_weight.transpose(1, 0, 2)
    patches = [pltpu.VMEM((27 * ins, CELLS), BF16), pltpu.VMEM((full, CELLS), BF16)]
    piece = ((ins, CELLS), BF16)
    hop = lambda v, step: lax.ppermute(v, "sample", [(s, s ^ step) for s in range(samples)])

    def chip_hops(parts):
        return [parts[0]] + [hop(parts[d], 2 * d) for d in range(1, chips)]

    cells = call(
        run(cells_kernel), [((ins, CELLS // chans), BF16)] * chans, [snapshots[0]], (), "cells", 0.5
    )
    cells = exchange(cells, chans)
    cots = exchange([cotangent[0]] * chans, chans)
    x, *parts = call(
        run(input_kernel), [piece] * (chans + 1), [first_w] + cells, patches, "first", 1.0
    )
    parts = exchange(parts, chans)
    full_cot = call(run(join_kernel), [((full, CELLS), BF16)], cots, (), "join", 0.5)[0]
    hidden_grad = call(
        spread_kernel, [((ins, CELLS), F32)], [second_w, full_cot], (), "spread", 1.5
    )[0]
    hidden, keep, give = call(
        run(gate_kernel),
        [piece, ((outs, CELLS), BF16), ((outs, CELLS), BF16)],
        [hidden_grad] + parts,
        [pltpu.VMEM((ins, CELLS), BF16)],
        "gate",
        0.9,
    )
    parts = call(
        run(output_kernel),
        [((2 * ins, CELLS), BF16)] * chans,
        [second_w, hidden, keep, hop(give, 1)],
        patches,
        "second",
        1.0,
    )
    hidden, *parts = lax.optimization_barrier((hidden, *parts))
    parts = exchange(parts, chans)
    pieces = call(
        pieces_kernel,
        [((chips, 3 * ins, CELLS), BF16)],
        [hidden, x, full_cot],
        (),
        "pieces",
        0.8,
    )[0]
    cores = [list(range(core, samples, 2)) for core in (0, 1)]
    pieces = lax.all_to_all(pieces, "sample", 0, 0, axis_index_groups=cores, tiled=True)
    routed = call(run(route_kernel), [piece] * chips, parts, patches[1:], "route", 0.6)
    pieces, *routed = lax.optimization_barrier((pieces, *routed))
    map_grads = chip_hops(routed)
    pieces = [pieces, hop(pieces, 1)]
    scratch = [
        pltpu.VMEM((9 * outs, samples * CELLS), BF16),
        pltpu.VMEM((3 * ins, samples * CELLS), BF16),
    ]
    out = [((27, outs, ins), F32)]
    second_grad = call(second_grad_kernel, out, pieces, scratch, "grad", 1.7)[0]
    second_grad, *parts = lax.optimization_barrier((second_grad, *parts))
    second_out = call(total_kernel, [piece], parts, (), "total", 0.5)[0]
    first_grad = call(first_grad_kernel, out, pieces + map_grads, scratch, "grad", 1.7)[0]
    return (
        second_out[None],
        first_grad.transpose(2, 0, 1),
        second_grad.transpose(2, 0, 1),
    )


def solution(mesh):
    placed = (
        P("sample", None, "chan"),
        P("chan", None, None),
        P("chan", None, None),
        P("sample", "chan", None),
    )
    samples, chans = mesh.shape["sample"], mesh.shape["chan"]
    square = samples == 2 * chans and chans in (2, 4)
    return jax.shard_map(
        functools.partial(body if square else plain_body, samples, chans),
        mesh=mesh,
        in_specs=placed,
        out_specs=(P("sample", "chan", None), P("chan", None, "sample"), P("chan", None, "sample")),
        check_vma=False,
    )
```

```python
import functools

import jax
import jax.numpy as jnp
from jax import lax
from jax.experimental import pallas as pl
from jax.experimental.pallas import tpu as pltpu
from jax.sharding import PartitionSpec as P

SIDE = 8
CELLS = SIDE**3
F32 = jnp.float32
BF16 = jnp.bfloat16
VMEM = pl.BlockSpec(memory_space=pltpu.VMEM)
TAPS = [(a, b, e) for a in (-1, 0, 1) for b in (-1, 0, 1) for e in (-1, 0, 1)]


def coords():
    cell = lax.broadcasted_iota(jnp.int32, (1, CELLS), 1)
    return cell >> 6, (cell >> 3) & 7, cell & 7


def moved(v, step):
    delta = 64 * step[0] + 8 * step[1] + step[2]
    if delta == 0:
        return v
    out = pltpu.roll(v, (-delta) % CELLS, 1)
    ok = None
    for at, by in zip(coords(), step):
        if by:
            good = at < SIDE - by if by > 0 else at >= -by
            ok = good if ok is None else ok & good
    return jnp.where(ok, out, jnp.zeros_like(out))


def call(kernel, outs, args, scratch=(), name=None, us=1.0):
    return pl.pallas_call(
        kernel,
        out_shape=[jax.ShapeDtypeStruct(shape, dtype) for shape, dtype in outs],
        in_specs=[VMEM] * len(args),
        out_specs=[VMEM] * len(outs),
        scratch_shapes=list(scratch),
        cost_estimate=pl.CostEstimate(
            flops=int(us * 1.1e9), bytes_accessed=int(us * 3.0e6), transcendentals=0
        ),
        compiler_params=pltpu.CompilerParams(vmem_limit_bytes=16 << 20),
        name=name,
    )(*args)


def block(j, chans, width):
    start = lax.rem(lax.axis_index("chan") + j, chans) * width
    return pl.ds(pl.multiple_of(start, width), width)


def split_kernel(chans, v_ref, g_ref, own, *outs):
    rows, width = own.shape
    own[...] = v_ref[block(0, chans, rows), :]
    for j, out in enumerate(outs):
        out[:, :width] = v_ref[block(j + 1, chans, rows), :]
        out[:, width:] = g_ref[...]


def conv_part(chans, w_ref, v, outs, patches, sums):
    rows = v.shape[0]
    for t, step in enumerate(TAPS):
        patches[t * rows : (t + 1) * rows, :] = moved(v, step)
    sums[...] = lax.dot_general(
        w_ref[...].reshape(-1, w_ref.shape[2]),
        patches[...],
        (((0,), (0,)), ((), ())),
        preferred_element_type=F32,
    ).astype(BF16)
    for j in range(chans):
        outs[j][...] = sums[block(j, chans, outs[j].shape[0]), :]


def first_kernel(chans, w_ref, own, g_ref, *refs):
    parts, (packed, full, *outs), scratch = refs[: chans - 1], refs[chans - 1 : -3], refs[-3:]
    x, *scratch = scratch
    rows, width = own.shape
    x[:, block(0, chans, width)] = own[...]
    full[block(0, chans, rows), :] = g_ref[...]
    for j, part in enumerate(parts):
        x[:, block(chans - j - 1, chans, width)] = part[:, :width]
        full[block(chans - j - 1, chans, rows), :] = part[:, width:]
    conv_part(chans, w_ref, x[...], outs, *scratch)
    fill(packed, x, full)


def fill(packed, x, full):
    rows = x.shape[0]
    outs = packed.shape[1] - rows
    for s in range(packed.shape[0]):
        packed[s, :rows, :] = x[...]
        packed[s, rows:, :] = full[s * outs : (s + 1) * outs, :]


def second_kernel(chans, w_ref, v_ref, *refs):
    conv_part(chans, w_ref, v_ref[...], refs[:chans], *refs[chans:])


def join_kernel(chans, *refs):
    parts, out = refs[:chans], refs[chans]
    rows = parts[0].shape[0]
    for j in range(chans):
        out[block(chans - j, chans, rows), :] = parts[j][...]


def pack_kernel(chans, x_ref, *refs):
    parts, (packed, full) = refs[:chans], refs[chans:]
    join_kernel(chans, *parts, full)
    fill(packed, x_ref, full)


def spread_kernel(w_ref, g_ref, o_ref):
    taps, rows, outs = w_ref.shape
    total = jnp.zeros((rows, CELLS), F32)
    for t, step in enumerate(TAPS):
        term = jnp.dot(w_ref[t], g_ref[...], preferred_element_type=F32)
        total = total + moved(term, tuple(-s for s in step))
    o_ref[...] = total


def middle_kernel(chans, hidden_grad, *refs):
    parts, (hidden_ref, copies_ref, map_grad_ref) = refs[:chans], refs[chans:]
    total = parts[0][...].astype(F32)
    for j in range(1, chans):
        total = total + parts[j][...].astype(F32)
    first_map = total.astype(BF16).astype(F32)
    gate = 1.0 / (1.0 + jnp.exp(-first_map))
    hidden = (first_map * gate).astype(BF16)
    hidden_ref[...] = hidden
    for s in range(copies_ref.shape[0]):
        copies_ref[s] = hidden
    map_grad_ref[...] = (hidden_grad[...] * gate * (1.0 + first_map * (1.0 - gate))).astype(BF16)


def grad_sum(pairs, o_ref, left, right):
    for n, (x, g) in enumerate(pairs):
        cells = pl.ds(n * CELLS, CELLS)
        ins, outs = x.shape[0], g.shape[0]
        for e in range(3):
            right[e * ins : (e + 1) * ins, cells] = moved(x, (0, 0, e - 1))
        for a in range(3):
            for b in range(3):
                row = (a * 3 + b) * outs
                left[row : row + outs, cells] = moved(g, (1 - a, 1 - b, 0))
    acc = lax.dot_general(
        left[...], right[...], (((1,), (1,)), ((), ())), preferred_element_type=F32
    )
    for ab in range(9):
        for e in range(3):
            o_ref[ab * 3 + e] = acc[ab * outs : (ab + 1) * outs, e * ins : (e + 1) * ins]


def grad_kernel(at, x_ref, g_ref, o_ref, left, right):
    ins = o_ref.shape[2]
    pairs = [(x_ref[n, :ins, :], g_ref[n, at:, :]) for n in range(x_ref.shape[0])]
    grad_sum(pairs, o_ref, left, right)


def grad(x, g, ins, at):
    count = x.shape[0]
    outs = g.shape[1] - at
    return call(
        functools.partial(grad_kernel, at),
        [((27, outs, ins), F32)],
        [x, g],
        [
            pltpu.VMEM((9 * outs, count * CELLS), BF16),
            pltpu.VMEM((3 * ins, count * CELLS), BF16),
        ],
        name="grad",
        us=3.0,
    )[0]


def swap(v, axis):
    return lax.all_to_all(v, axis, 0, 0, tiled=True)


def send(v, step, size):
    return lax.ppermute(v, "chan", [(k, (k + step) % size) for k in range(size)])


def exchange(parts, size):
    return [parts[0]] + [send(parts[j], j, size) for j in range(1, size)]


def plain_body(samples, chans, snapshots, first_weight, second_weight, cotangent):
    ins = first_weight.shape[0]
    full = snapshots.shape[1]
    outs = full // samples
    width = CELLS // chans
    run = lambda kernel: functools.partial(kernel, chans)
    first_w = first_weight.transpose(1, 0, 2)
    second_w = second_weight.transpose(1, 0, 2)
    patches = [pltpu.VMEM((27 * ins, CELLS), BF16), pltpu.VMEM((full, CELLS), BF16)]
    piece = ((ins, CELLS), BF16)

    gathered = [((samples, ins + outs, CELLS), BF16), ((full, CELLS), BF16)]
    if width % 128 == 0:
        cells = [((ins, width), BF16)] + [((ins, width + CELLS), BF16)] * (chans - 1)
        cells = call(run(split_kernel), cells, [snapshots[0], cotangent[0]], name="split")
        own, *cells = exchange(cells, chans)
        packed, full_cot, *parts = call(
            run(first_kernel),
            gathered + [piece] * chans,
            [first_w, own, cotangent[0]] + cells,
            [pltpu.VMEM((ins, CELLS), BF16)] + patches,
            "first",
            3.0,
        )
    else:
        x = swap(snapshots[0].reshape(chans, ins, width), "chan")
        x = x.transpose(1, 0, 2).reshape(ins, CELLS)
        parts = call(run(second_kernel), [piece] * chans, [first_w, x], patches, "first", 2.8)
        cots = exchange([cotangent[0]] * chans, chans)
        packed, full_cot = call(run(pack_kernel), gathered, [x] + cots, name="pack")
    parts = exchange(parts, chans)
    packed = swap(packed, "sample")
    hidden_grad = call(spread_kernel, [((ins, CELLS), F32)], [second_w, full_cot], (), "spread", 3.4)[0]
    hidden, copies, map_grad = call(
        run(middle_kernel),
        [piece, ((samples, ins, CELLS), BF16), piece],
        [hidden_grad] + parts,
        name="middle",
        us=2.0,
    )
    copies, packed = lax.optimization_barrier((copies, packed))
    all_hidden = swap(copies, "sample")
    map_grads = exchange([map_grad] * chans, chans)
    parts = exchange(
        call(run(second_kernel), [piece] * chans, [second_w, hidden], patches, "second", 2.8), chans
    )
    full_map_grad = call(run(join_kernel), [((full, CELLS), BF16)], map_grads, name="join")[0]
    full_map_grad, all_hidden = lax.optimization_barrier((full_map_grad, all_hidden))
    all_map_grad = swap(full_map_grad.reshape(samples, outs, CELLS), "sample")
    second_out = sum(p.astype(F32) for p in parts).astype(BF16)
    second_grad = grad(all_hidden, packed, ins, ins)
    first_grad = grad(packed, all_map_grad, ins, 0)
    return (
        second_out[None],
        first_grad.transpose(2, 0, 1),
        second_grad.transpose(2, 0, 1),
    )


def half(rows):
    return pl.ds(pl.multiple_of((lax.axis_index("sample") & 1) * rows, rows), rows)


def far(step, rows):
    chip = (lax.axis_index("sample") >> 1) ^ step
    return pl.ds(pl.multiple_of(chip * rows, rows), rows)


def cells_kernel(chans, v_ref, *outs):
    for j, out in enumerate(outs):
        out[...] = v_ref[block(j, chans, out.shape[0]), :]


def input_kernel(chans, w_ref, *refs):
    parts, (x, *outs), scratch = refs[:chans], refs[chans:-2], refs[-2:]
    for j, part in enumerate(parts):
        x[:, block(chans - j, chans, part.shape[1])] = part[...]
    conv_part(chans, w_ref, x[...], outs, *scratch)


def pieces_kernel(hidden, x, full, out):
    rows = x.shape[0]
    for chip in range(out.shape[0]):
        out[chip, :rows, :] = hidden[...]
        out[chip, rows : 2 * rows, :] = x[...]
        out[chip, 2 * rows :, :] = full[chip * rows : (chip + 1) * rows, :]


def gate_kernel(chans, hidden_grad, *refs):
    parts, (hidden_ref, keep, give, both) = refs[:chans], refs[chans:]
    total = parts[0][...].astype(F32)
    for j in range(1, chans):
        total = total + parts[j][...].astype(F32)
    first_map = total.astype(BF16).astype(F32)
    gate = 1.0 / (1.0 + jnp.exp(-first_map))
    hidden_ref[...] = (first_map * gate).astype(BF16)
    both[...] = (hidden_grad[...] * gate * (1.0 + first_map * (1.0 - gate))).astype(BF16)
    rows = keep.shape[0]
    keep[...] = both[half(rows), :]
    other = pl.multiple_of((1 - (lax.axis_index("sample") & 1)) * rows, rows)
    give[...] = both[pl.ds(other, rows), :]


def stack_kernel(top, bottom, out):
    rows = top.shape[0]
    out[:rows, :] = top[...]
    out[rows:, :] = bottom[...]


def route_kernel(chans, *refs):
    parts, outs, full = refs[:chans], refs[chans:-1], refs[-1]
    rows = outs[0].shape[0]
    join_kernel(chans, *parts, full)
    for step, out in enumerate(outs):
        out[...] = full[far(step, rows), :]


def total_kernel(*refs):
    *parts, out = refs
    total = parts[0][...].astype(F32)
    for part in parts[1:]:
        total = total + part[...].astype(F32)
    out[...] = total.astype(BF16)


def second_grad_kernel(mine, other, *rest):
    rows, ins = rest[0].shape[1:]
    start = pl.multiple_of(2 * ins + (lax.axis_index("sample") & 1) * rows, rows)
    pairs = []
    for chip in range(mine.shape[0]):
        for v in (mine, other):
            pairs.append((v[chip, :ins, :], v[chip, pl.ds(start, rows), :]))
    grad_sum(pairs, *rest)


def first_grad_kernel(mine, other, *refs):
    maps, rest = refs[:-3], refs[-3:]
    rows, ins = rest[0].shape[1:]
    pairs = []
    for step, g in enumerate(maps):
        chip = (lax.axis_index("sample") >> 1) ^ step
        for core, v in enumerate((mine, other)):
            at = core * rows
            pairs.append((v[chip, ins : 2 * ins, :], g[at : at + rows, :]))
    grad_sum(pairs, *rest)


def body(samples, chans, snapshots, first_weight, second_weight, cotangent):
    ins = first_weight.shape[0]
    full = snapshots.shape[1]
    outs = full // samples
    chips = samples // 2
    run = lambda kernel: functools.partial(kernel, chans)
    first_w = first_weight.transpose(1, 0, 2)
    second_w = second_weight.transpose(1, 0, 2)
    patches = [pltpu.VMEM((27 * ins, CELLS), BF16), pltpu.VMEM((full, CELLS), BF16)]
    piece = ((ins, CELLS), BF16)
    hop = lambda v, step: lax.ppermute(v, "sample", [(s, s ^ step) for s in range(samples)])

    def chip_hops(parts):
        return [parts[0]] + [hop(parts[d], 2 * d) for d in range(1, chips)]

    cells = call(
        run(cells_kernel), [((ins, CELLS // chans), BF16)] * chans, [snapshots[0]], (), "cells", 0.5
    )
    cells = exchange(cells, chans)
    cots = exchange([cotangent[0]] * chans, chans)
    x, *parts = call(
        run(input_kernel), [piece] * (chans + 1), [first_w] + cells, patches, "first", 1.0
    )
    parts = exchange(parts, chans)
    full_cot = call(run(join_kernel), [((full, CELLS), BF16)], cots, (), "join", 0.5)[0]
    hidden_grad = call(
        spread_kernel, [((ins, CELLS), F32)], [second_w, full_cot], (), "spread", 1.5
    )[0]
    hidden, keep, give = call(
        run(gate_kernel),
        [piece, ((outs, CELLS), BF16), ((outs, CELLS), BF16)],
        [hidden_grad] + parts,
        [pltpu.VMEM((ins, CELLS), BF16)],
        "gate",
        0.9,
    )
    got = hop(give, 1)
    map_grad = call(stack_kernel, [piece], [keep, got], (), "stack", 0.3)[0]
    map_grads = exchange([map_grad] * chans, chans)
    parts = exchange(
        call(run(second_kernel), [piece] * chans, [second_w, hidden], patches, "second", 0.9), chans
    )
    pieces = call(
        pieces_kernel,
        [((chips, 3 * ins, CELLS), BF16)],
        [hidden, x, full_cot],
        (),
        "pieces",
        0.8,
    )[0]
    pieces, got = lax.optimization_barrier((pieces, got))
    cores = [list(range(core, samples, 2)) for core in (0, 1)]
    pieces = lax.all_to_all(pieces, "sample", 0, 0, axis_index_groups=cores, tiled=True)
    routed = call(run(route_kernel), [piece] * chips, map_grads, patches[1:], "route", 15.0)
    map_grads = chip_hops(routed)
    pieces = [pieces, hop(pieces, 1)]
    scratch = [
        pltpu.VMEM((9 * outs, samples * CELLS), BF16),
        pltpu.VMEM((3 * ins, samples * CELLS), BF16),
    ]
    out = [((27, outs, ins), F32)]
    second_grad = call(second_grad_kernel, out, pieces, scratch, "grad", 1.7)[0]
    second_grad, *parts = lax.optimization_barrier((second_grad, *parts))
    second_out = call(total_kernel, [piece], parts, (), "total", 0.5)[0]
    first_grad = call(first_grad_kernel, out, pieces + map_grads, scratch, "grad", 1.7)[0]
    return (
        second_out[None],
        first_grad.transpose(2, 0, 1),
        second_grad.transpose(2, 0, 1),
    )


def solution(mesh):
    placed = (
        P("sample", None, "chan"),
        P("chan", None, None),
        P("chan", None, None),
        P("sample", "chan", None),
    )
    samples, chans = mesh.shape["sample"], mesh.shape["chan"]
    square = samples == 2 * chans and chans in (2, 4)
    return jax.shard_map(
        functools.partial(body if square else plain_body, samples, chans),
        mesh=mesh,
        in_specs=placed,
        out_specs=(P("sample", "chan", None), P("chan", None, "sample"), P("chan", None, "sample")),
        check_vma=False,
    )
```

```python
import functools

import jax
import jax.numpy as jnp
from jax import lax
from jax.experimental import pallas as pl
from jax.experimental.pallas import tpu as pltpu
from jax.sharding import PartitionSpec as P

SIDE = 8
CELLS = SIDE**3
F32 = jnp.float32
BF16 = jnp.bfloat16
VMEM = pl.BlockSpec(memory_space=pltpu.VMEM)
TAPS = [(a, b, e) for a in (-1, 0, 1) for b in (-1, 0, 1) for e in (-1, 0, 1)]


def coords():
    cell = lax.broadcasted_iota(jnp.int32, (1, CELLS), 1)
    return cell >> 6, (cell >> 3) & 7, cell & 7


def moved(v, step):
    delta = 64 * step[0] + 8 * step[1] + step[2]
    if delta == 0:
        return v
    out = pltpu.roll(v, (-delta) % CELLS, 1)
    ok = None
    for at, by in zip(coords(), step):
        if by:
            good = at < SIDE - by if by > 0 else at >= -by
            ok = good if ok is None else ok & good
    return jnp.where(ok, out, jnp.zeros_like(out))


def call(kernel, outs, args, scratch=(), name=None, us=1.0):
    return pl.pallas_call(
        kernel,
        out_shape=[jax.ShapeDtypeStruct(shape, dtype) for shape, dtype in outs],
        in_specs=[VMEM] * len(args),
        out_specs=[VMEM] * len(outs),
        scratch_shapes=list(scratch),
        cost_estimate=pl.CostEstimate(
            flops=int(us * 1.1e9), bytes_accessed=int(us * 3.0e6), transcendentals=0
        ),
        compiler_params=pltpu.CompilerParams(vmem_limit_bytes=16 << 20),
        name=name,
    )(*args)


def block(j, chans, width):
    start = lax.rem(lax.axis_index("chan") + j, chans) * width
    return pl.ds(pl.multiple_of(start, width), width)


def split_kernel(chans, v_ref, g_ref, own, *outs):
    rows, width = own.shape
    own[...] = v_ref[block(0, chans, rows), :]
    for j, out in enumerate(outs):
        out[:, :width] = v_ref[block(j + 1, chans, rows), :]
        out[:, width:] = g_ref[...]


def conv_part(chans, w_ref, v, outs, patches, sums):
    rows = v.shape[0]
    for t, step in enumerate(TAPS):
        patches[t * rows : (t + 1) * rows, :] = moved(v, step)
    sums[...] = lax.dot_general(
        w_ref[...].reshape(-1, w_ref.shape[2]),
        patches[...],
        (((0,), (0,)), ((), ())),
        preferred_element_type=F32,
    ).astype(BF16)
    for j in range(chans):
        outs[j][...] = sums[block(j, chans, outs[j].shape[0]), :]


def first_kernel(chans, w_ref, own, g_ref, *refs):
    parts, (packed, full, *outs), scratch = refs[: chans - 1], refs[chans - 1 : -3], refs[-3:]
    x, *scratch = scratch
    rows, width = own.shape
    x[:, block(0, chans, width)] = own[...]
    full[block(0, chans, rows), :] = g_ref[...]
    for j, part in enumerate(parts):
        x[:, block(chans - j - 1, chans, width)] = part[:, :width]
        full[block(chans - j - 1, chans, rows), :] = part[:, width:]
    conv_part(chans, w_ref, x[...], outs, *scratch)
    fill(packed, x, full)


def fill(packed, x, full):
    rows = x.shape[0]
    outs = packed.shape[1] - rows
    for s in range(packed.shape[0]):
        packed[s, :rows, :] = x[...]
        packed[s, rows:, :] = full[s * outs : (s + 1) * outs, :]


def second_kernel(chans, w_ref, v_ref, *refs):
    conv_part(chans, w_ref, v_ref[...], refs[:chans], *refs[chans:])


def join_kernel(chans, *refs):
    parts, out = refs[:chans], refs[chans]
    rows = parts[0].shape[0]
    for j in range(chans):
        out[block(chans - j, chans, rows), :] = parts[j][...]


def pack_kernel(chans, x_ref, *refs):
    parts, (packed, full) = refs[:chans], refs[chans:]
    join_kernel(chans, *parts, full)
    fill(packed, x_ref, full)


def spread_kernel(w_ref, g_ref, o_ref):
    taps, rows, outs = w_ref.shape
    total = jnp.zeros((rows, CELLS), F32)
    for t, step in enumerate(TAPS):
        term = jnp.dot(w_ref[t], g_ref[...], preferred_element_type=F32)
        total = total + moved(term, tuple(-s for s in step))
    o_ref[...] = total


def middle_kernel(chans, hidden_grad, *refs):
    parts, (hidden_ref, copies_ref, map_grad_ref) = refs[:chans], refs[chans:]
    total = parts[0][...].astype(F32)
    for j in range(1, chans):
        total = total + parts[j][...].astype(F32)
    first_map = total.astype(BF16).astype(F32)
    gate = 1.0 / (1.0 + jnp.exp(-first_map))
    hidden = (first_map * gate).astype(BF16)
    hidden_ref[...] = hidden
    for s in range(copies_ref.shape[0]):
        copies_ref[s] = hidden
    map_grad_ref[...] = (hidden_grad[...] * gate * (1.0 + first_map * (1.0 - gate))).astype(BF16)


def grad_sum(pairs, o_ref, left, right, begin=None):
    for n, (x, g) in enumerate(pairs):
        cells = pl.ds(n * CELLS, CELLS)
        ins, outs = x.shape[0], g.shape[0]
        for e in range(3):
            right[e * ins : (e + 1) * ins, cells] = moved(x, (0, 0, e - 1))
        for a in range(3):
            for b in range(3):
                row = (a * 3 + b) * outs
                left[row : row + outs, cells] = moved(g, (1 - a, 1 - b, 0))
    acc = lax.dot_general(
        left[...], right[...], (((1,), (1,)), ((), ())), preferred_element_type=F32
    )
    for ab in range(9):
        for e in range(3):
            out = acc[ab * outs : (ab + 1) * outs, e * ins : (e + 1) * ins]
            o_ref[ab * 3 + e] = out if begin is None else out + begin[ab * 3 + e]


def grad_kernel(at, x_ref, g_ref, o_ref, left, right):
    ins = o_ref.shape[2]
    pairs = [(x_ref[n, :ins, :], g_ref[n, at:, :]) for n in range(x_ref.shape[0])]
    grad_sum(pairs, o_ref, left, right)


def grad(x, g, ins, at):
    count = x.shape[0]
    outs = g.shape[1] - at
    return call(
        functools.partial(grad_kernel, at),
        [((27, outs, ins), F32)],
        [x, g],
        [
            pltpu.VMEM((9 * outs, count * CELLS), BF16),
            pltpu.VMEM((3 * ins, count * CELLS), BF16),
        ],
        name="grad",
        us=3.0,
    )[0]


def swap(v, axis):
    return lax.all_to_all(v, axis, 0, 0, tiled=True)


def send(v, step, size):
    return lax.ppermute(v, "chan", [(k, (k + step) % size) for k in range(size)])


def exchange(parts, size):
    return [parts[0]] + [send(parts[j], j, size) for j in range(1, size)]


def plain_body(samples, chans, snapshots, first_weight, second_weight, cotangent):
    ins = first_weight.shape[0]
    full = snapshots.shape[1]
    outs = full // samples
    width = CELLS // chans
    run = lambda kernel: functools.partial(kernel, chans)
    first_w = first_weight.transpose(1, 0, 2)
    second_w = second_weight.transpose(1, 0, 2)
    patches = [pltpu.VMEM((27 * ins, CELLS), BF16), pltpu.VMEM((full, CELLS), BF16)]
    piece = ((ins, CELLS), BF16)

    gathered = [((samples, ins + outs, CELLS), BF16), ((full, CELLS), BF16)]
    if width % 128 == 0:
        cells = [((ins, width), BF16)] + [((ins, width + CELLS), BF16)] * (chans - 1)
        cells = call(run(split_kernel), cells, [snapshots[0], cotangent[0]], name="split")
        own, *cells = exchange(cells, chans)
        packed, full_cot, *parts = call(
            run(first_kernel),
            gathered + [piece] * chans,
            [first_w, own, cotangent[0]] + cells,
            [pltpu.VMEM((ins, CELLS), BF16)] + patches,
            "first",
            3.0,
        )
    else:
        x = swap(snapshots[0].reshape(chans, ins, width), "chan")
        x = x.transpose(1, 0, 2).reshape(ins, CELLS)
        parts = call(run(second_kernel), [piece] * chans, [first_w, x], patches, "first", 2.8)
        cots = exchange([cotangent[0]] * chans, chans)
        packed, full_cot = call(run(pack_kernel), gathered, [x] + cots, name="pack")
    parts = exchange(parts, chans)
    packed = swap(packed, "sample")
    hidden_grad = call(spread_kernel, [((ins, CELLS), F32)], [second_w, full_cot], (), "spread", 3.4)[0]
    hidden, copies, map_grad = call(
        run(middle_kernel),
        [piece, ((samples, ins, CELLS), BF16), piece],
        [hidden_grad] + parts,
        name="middle",
        us=2.0,
    )
    copies, packed = lax.optimization_barrier((copies, packed))
    all_hidden = swap(copies, "sample")
    map_grads = exchange([map_grad] * chans, chans)
    parts = exchange(
        call(run(second_kernel), [piece] * chans, [second_w, hidden], patches, "second", 2.8), chans
    )
    full_map_grad = call(run(join_kernel), [((full, CELLS), BF16)], map_grads, name="join")[0]
    full_map_grad, all_hidden = lax.optimization_barrier((full_map_grad, all_hidden))
    all_map_grad = swap(full_map_grad.reshape(samples, outs, CELLS), "sample")
    second_out = sum(p.astype(F32) for p in parts).astype(BF16)
    second_grad = grad(all_hidden, packed, ins, ins)
    first_grad = grad(packed, all_map_grad, ins, 0)
    return (
        second_out[None],
        first_grad.transpose(2, 0, 1),
        second_grad.transpose(2, 0, 1),
    )


def half(rows):
    return pl.ds(pl.multiple_of((lax.axis_index("sample") & 1) * rows, rows), rows)


def far(step, rows):
    chip = (lax.axis_index("sample") >> 1) ^ step
    return pl.ds(pl.multiple_of(chip * rows, rows), rows)


def cells_kernel(chans, v_ref, *outs):
    for j, out in enumerate(outs):
        out[...] = v_ref[block(j, chans, out.shape[0]), :]


def input_kernel(chans, w_ref, *refs):
    parts, (x, *outs), scratch = refs[:chans], refs[chans:-2], refs[-2:]
    for j, part in enumerate(parts):
        x[:, block(chans - j, chans, part.shape[1])] = part[...]
    conv_part(chans, w_ref, x[...], outs, *scratch)


def pieces_kernel(hidden, x, full, out):
    rows = x.shape[0]
    for chip in range(out.shape[0]):
        out[chip, :rows, :] = hidden[...]
        out[chip, rows : 2 * rows, :] = x[...]
        out[chip, 2 * rows :, :] = full[chip * rows : (chip + 1) * rows, :]


def gate_kernel(chans, hidden_grad, *refs):
    parts, (hidden_ref, keep, give, both) = refs[:chans], refs[chans:]
    total = parts[0][...].astype(F32)
    for j in range(1, chans):
        total = total + parts[j][...].astype(F32)
    first_map = total.astype(BF16).astype(F32)
    gate = 1.0 / (1.0 + jnp.exp(-first_map))
    hidden_ref[...] = (first_map * gate).astype(BF16)
    both[...] = (hidden_grad[...] * gate * (1.0 + first_map * (1.0 - gate))).astype(BF16)
    rows = keep.shape[0]
    keep[...] = both[half(rows), :]
    other = pl.multiple_of((1 - (lax.axis_index("sample") & 1)) * rows, rows)
    give[...] = both[pl.ds(other, rows), :]


def stack_kernel(top, bottom, out):
    rows = top.shape[0]
    out[:rows, :] = top[...]
    out[rows:, :] = bottom[...]


def route_kernel(chans, *refs):
    parts, outs, full = refs[:chans], refs[chans:-1], refs[-1]
    rows = outs[0].shape[0]
    join_kernel(chans, *parts, full)
    for step, out in enumerate(outs):
        out[...] = full[far(step, rows), :]


def total_kernel(*refs):
    *parts, out = refs
    total = parts[0][...].astype(F32)
    for part in parts[1:]:
        total = total + part[...].astype(F32)
    out[...] = total.astype(BF16)


def second_grad_kernel(mine, other, *rest):
    rows, ins = rest[0].shape[1:]
    start = pl.multiple_of(2 * ins + (lax.axis_index("sample") & 1) * rows, rows)
    pairs = []
    for chip in range(mine.shape[0]):
        for v in (mine, other):
            pairs.append((v[chip, :ins, :], v[chip, pl.ds(start, rows), :]))
    grad_sum(pairs, *rest)


def first_grad_kernel(steps, mine, other, *refs):
    count = len(steps)
    maps, begin, rest = refs[:count], refs[count:-3], refs[-3:]
    rows, ins = rest[0].shape[1:]
    pairs = []
    for step, g in zip(steps, maps):
        chip = (lax.axis_index("sample") >> 1) ^ step
        for core, v in enumerate((mine, other)):
            at = core * rows
            pairs.append((v[chip, ins : 2 * ins, :], g[at : at + rows, :]))
    grad_sum(pairs, *rest, *begin)


def body(samples, chans, snapshots, first_weight, second_weight, cotangent):
    ins = first_weight.shape[0]
    full = snapshots.shape[1]
    outs = full // samples
    chips = samples // 2
    run = lambda kernel: functools.partial(kernel, chans)
    first_w = first_weight.transpose(1, 0, 2)
    second_w = second_weight.transpose(1, 0, 2)
    patches = [pltpu.VMEM((27 * ins, CELLS), BF16), pltpu.VMEM((full, CELLS), BF16)]
    piece = ((ins, CELLS), BF16)
    hop = lambda v, step: lax.ppermute(v, "sample", [(s, s ^ step) for s in range(samples)])

    def chip_hops(parts):
        return [parts[0]] + [hop(parts[d], 2 * d) for d in range(1, chips)]

    cells = call(
        run(cells_kernel), [((ins, CELLS // chans), BF16)] * chans, [snapshots[0]], (), "cells", 0.5
    )
    cells = exchange(cells, chans)
    cots = exchange([cotangent[0]] * chans, chans)
    cots[1], *cells = lax.optimization_barrier((cots[1], *cells))
    x, *parts = call(
        run(input_kernel), [piece] * (chans + 1), [first_w] + cells, patches, "first", 1.0
    )
    parts = exchange(parts, chans)
    full_cot = call(run(join_kernel), [((full, CELLS), BF16)], cots, (), "join", 0.5)[0]
    hidden_grad = call(
        spread_kernel, [((ins, CELLS), F32)], [second_w, full_cot], (), "spread", 1.5
    )[0]
    hidden, keep, give = call(
        run(gate_kernel),
        [piece, ((outs, CELLS), BF16), ((outs, CELLS), BF16)],
        [hidden_grad] + parts,
        [pltpu.VMEM((ins, CELLS), BF16)],
        "gate",
        0.9,
    )
    got = hop(give, 1)
    map_grad = call(stack_kernel, [piece], [keep, got], (), "stack", 0.3)[0]
    map_grads = exchange([map_grad] * chans, chans)
    parts = exchange(
        call(run(second_kernel), [piece] * chans, [second_w, hidden], patches, "second", 0.9), chans
    )
    pieces = call(
        pieces_kernel,
        [((chips, 3 * ins, CELLS), BF16)],
        [hidden, x, full_cot],
        (),
        "pieces",
        0.8,
    )[0]
    pieces, got = lax.optimization_barrier((pieces, got))
    cores = [list(range(core, samples, 2)) for core in (0, 1)]
    pieces = lax.all_to_all(pieces, "sample", 0, 0, axis_index_groups=cores, tiled=True)
    routed = call(run(route_kernel), [piece] * chips, map_grads, patches[1:], "route", 15.0)
    map_grads = chip_hops(routed)
    pieces = [pieces, hop(pieces, 1)]
    def grad_call(kernel, args, count):
        scratch = [
            pltpu.VMEM((9 * outs, count * CELLS), BF16),
            pltpu.VMEM((3 * ins, count * CELLS), BF16),
        ]
        us = 0.3
        return call(kernel, [((27, outs, ins), F32)], args, scratch, "grad", us)[0]

    second_grad = grad_call(second_grad_kernel, pieces, samples)
    second_grad, *parts = lax.optimization_barrier((second_grad, *parts))
    second_out = call(total_kernel, [piece], parts, (), "total", 0.1)[0]
    first_grad = []
    for steps in (range(chips - 1), [chips - 1]):
        args = pieces + [map_grads[d] for d in steps] + first_grad
        kernel = functools.partial(first_grad_kernel, tuple(steps))
        first_grad = [grad_call(kernel, args, 2 * len(steps))]
    first_grad = first_grad[0]
    return (
        second_out[None],
        first_grad.transpose(2, 0, 1),
        second_grad.transpose(2, 0, 1),
    )


def solution(mesh):
    placed = (
        P("sample", None, "chan"),
        P("chan", None, None),
        P("chan", None, None),
        P("sample", "chan", None),
    )
    samples, chans = mesh.shape["sample"], mesh.shape["chan"]
    square = samples == 2 * chans and chans in (2, 4)
    return jax.shard_map(
        functools.partial(body if square else plain_body, samples, chans),
        mesh=mesh,
        in_specs=placed,
        out_specs=(P("sample", "chan", None), P("chan", None, "sample"), P("chan", None, "sample")),
        check_vma=False,
    )
```

```python
import functools

import jax
import jax.numpy as jnp
from jax import lax
from jax.experimental import pallas as pl
from jax.experimental.pallas import tpu as pltpu
from jax.sharding import PartitionSpec as P

SIDE = 8
CELLS = SIDE**3
F32 = jnp.float32
BF16 = jnp.bfloat16
VMEM = pl.BlockSpec(memory_space=pltpu.VMEM)
TAPS = [(a, b, e) for a in (-1, 0, 1) for b in (-1, 0, 1) for e in (-1, 0, 1)]


def coords():
    cell = lax.broadcasted_iota(jnp.int32, (1, CELLS), 1)
    return cell >> 6, (cell >> 3) & 7, cell & 7


def moved(v, step):
    delta = 64 * step[0] + 8 * step[1] + step[2]
    if delta == 0:
        return v
    out = pltpu.roll(v, (-delta) % CELLS, 1)
    ok = None
    for at, by in zip(coords(), step):
        if by:
            good = at < SIDE - by if by > 0 else at >= -by
            ok = good if ok is None else ok & good
    return jnp.where(ok, out, jnp.zeros_like(out))


def call(kernel, outs, args, scratch=(), name=None, us=1.0):
    return pl.pallas_call(
        kernel,
        out_shape=[jax.ShapeDtypeStruct(shape, dtype) for shape, dtype in outs],
        in_specs=[VMEM] * len(args),
        out_specs=[VMEM] * len(outs),
        scratch_shapes=list(scratch),
        cost_estimate=pl.CostEstimate(
            flops=int(us * 1.1e9), bytes_accessed=int(us * 3.0e6), transcendentals=0
        ),
        compiler_params=pltpu.CompilerParams(vmem_limit_bytes=16 << 20),
        name=name,
    )(*args)


def block(j, chans, width):
    start = lax.rem(lax.axis_index("chan") + j, chans) * width
    return pl.ds(pl.multiple_of(start, width), width)


def split_kernel(chans, v_ref, g_ref, own, *outs):
    rows, width = own.shape
    own[...] = v_ref[block(0, chans, rows), :]
    for j, out in enumerate(outs):
        out[:, :width] = v_ref[block(j + 1, chans, rows), :]
        out[:, width:] = g_ref[...]


def conv_part(chans, w_ref, v, outs, patches, sums):
    rows = v.shape[0]
    for t, step in enumerate(TAPS):
        patches[t * rows : (t + 1) * rows, :] = moved(v, step)
    sums[...] = lax.dot_general(
        w_ref[...].reshape(-1, w_ref.shape[2]),
        patches[...],
        (((0,), (0,)), ((), ())),
        preferred_element_type=F32,
    ).astype(BF16)
    for j in range(chans):
        outs[j][...] = sums[block(j, chans, outs[j].shape[0]), :]


def first_kernel(chans, w_ref, own, g_ref, *refs):
    parts, (packed, full, *outs), scratch = refs[: chans - 1], refs[chans - 1 : -3], refs[-3:]
    x, *scratch = scratch
    rows, width = own.shape
    x[:, block(0, chans, width)] = own[...]
    full[block(0, chans, rows), :] = g_ref[...]
    for j, part in enumerate(parts):
        x[:, block(chans - j - 1, chans, width)] = part[:, :width]
        full[block(chans - j - 1, chans, rows), :] = part[:, width:]
    conv_part(chans, w_ref, x[...], outs, *scratch)
    fill(packed, x, full)


def fill(packed, x, full):
    rows = x.shape[0]
    outs = packed.shape[1] - rows
    for s in range(packed.shape[0]):
        packed[s, :rows, :] = x[...]
        packed[s, rows:, :] = full[s * outs : (s + 1) * outs, :]


def second_kernel(chans, w_ref, v_ref, *refs):
    conv_part(chans, w_ref, v_ref[...], refs[:chans], *refs[chans:])


def join_kernel(chans, *refs):
    parts, out = refs[:chans], refs[chans]
    rows = parts[0].shape[0]
    for j in range(chans):
        out[block(chans - j, chans, rows), :] = parts[j][...]


def pack_kernel(chans, x_ref, *refs):
    parts, (packed, full) = refs[:chans], refs[chans:]
    join_kernel(chans, *parts, full)
    fill(packed, x_ref, full)


def spread_kernel(w_ref, g_ref, o_ref):
    taps, rows, outs = w_ref.shape
    total = jnp.zeros((rows, CELLS), F32)
    for t, step in enumerate(TAPS):
        term = jnp.dot(w_ref[t], g_ref[...], preferred_element_type=F32)
        total = total + moved(term, tuple(-s for s in step))
    o_ref[...] = total


def middle_kernel(chans, hidden_grad, *refs):
    parts, (hidden_ref, copies_ref, map_grad_ref) = refs[:chans], refs[chans:]
    total = parts[0][...].astype(F32)
    for j in range(1, chans):
        total = total + parts[j][...].astype(F32)
    first_map = total.astype(BF16).astype(F32)
    gate = 1.0 / (1.0 + jnp.exp(-first_map))
    hidden = (first_map * gate).astype(BF16)
    hidden_ref[...] = hidden
    for s in range(copies_ref.shape[0]):
        copies_ref[s] = hidden
    map_grad_ref[...] = (hidden_grad[...] * gate * (1.0 + first_map * (1.0 - gate))).astype(BF16)


def grad_sum(pairs, o_ref, left, right, begin=None):
    for n, (x, g) in enumerate(pairs):
        cells = pl.ds(n * CELLS, CELLS)
        ins, outs = x.shape[0], g.shape[0]
        for e in range(3):
            right[e * ins : (e + 1) * ins, cells] = moved(x, (0, 0, e - 1))
        for a in range(3):
            for b in range(3):
                row = (a * 3 + b) * outs
                left[row : row + outs, cells] = moved(g, (1 - a, 1 - b, 0))
    acc = lax.dot_general(
        left[...], right[...], (((1,), (1,)), ((), ())), preferred_element_type=F32
    )
    for ab in range(9):
        for e in range(3):
            out = acc[ab * outs : (ab + 1) * outs, e * ins : (e + 1) * ins]
            o_ref[ab * 3 + e] = out if begin is None else out + begin[ab * 3 + e]


def grad_kernel(at, x_ref, g_ref, o_ref, left, right):
    ins = o_ref.shape[2]
    pairs = [(x_ref[n, :ins, :], g_ref[n, at:, :]) for n in range(x_ref.shape[0])]
    grad_sum(pairs, o_ref, left, right)


def grad(x, g, ins, at):
    count = x.shape[0]
    outs = g.shape[1] - at
    return call(
        functools.partial(grad_kernel, at),
        [((27, outs, ins), F32)],
        [x, g],
        [
            pltpu.VMEM((9 * outs, count * CELLS), BF16),
            pltpu.VMEM((3 * ins, count * CELLS), BF16),
        ],
        name="grad",
        us=3.0,
    )[0]


def swap(v, axis):
    return lax.all_to_all(v, axis, 0, 0, tiled=True)


def send(v, step, size):
    return lax.ppermute(v, "chan", [(k, (k + step) % size) for k in range(size)])


def exchange(parts, size):
    return [parts[0]] + [send(parts[j], j, size) for j in range(1, size)]


def plain_body(samples, chans, snapshots, first_weight, second_weight, cotangent):
    ins = first_weight.shape[0]
    full = snapshots.shape[1]
    outs = full // samples
    width = CELLS // chans
    run = lambda kernel: functools.partial(kernel, chans)
    first_w = first_weight.transpose(1, 0, 2)
    second_w = second_weight.transpose(1, 0, 2)
    patches = [pltpu.VMEM((27 * ins, CELLS), BF16), pltpu.VMEM((full, CELLS), BF16)]
    piece = ((ins, CELLS), BF16)

    gathered = [((samples, ins + outs, CELLS), BF16), ((full, CELLS), BF16)]
    if width % 128 == 0:
        cells = [((ins, width), BF16)] + [((ins, width + CELLS), BF16)] * (chans - 1)
        cells = call(run(split_kernel), cells, [snapshots[0], cotangent[0]], name="split")
        own, *cells = exchange(cells, chans)
        packed, full_cot, *parts = call(
            run(first_kernel),
            gathered + [piece] * chans,
            [first_w, own, cotangent[0]] + cells,
            [pltpu.VMEM((ins, CELLS), BF16)] + patches,
            "first",
            3.0,
        )
    else:
        x = swap(snapshots[0].reshape(chans, ins, width), "chan")
        x = x.transpose(1, 0, 2).reshape(ins, CELLS)
        parts = call(run(second_kernel), [piece] * chans, [first_w, x], patches, "first", 2.8)
        cots = exchange([cotangent[0]] * chans, chans)
        packed, full_cot = call(run(pack_kernel), gathered, [x] + cots, name="pack")
    parts = exchange(parts, chans)
    packed = swap(packed, "sample")
    hidden_grad = call(spread_kernel, [((ins, CELLS), F32)], [second_w, full_cot], (), "spread", 3.4)[0]
    hidden, copies, map_grad = call(
        run(middle_kernel),
        [piece, ((samples, ins, CELLS), BF16), piece],
        [hidden_grad] + parts,
        name="middle",
        us=2.0,
    )
    copies, packed = lax.optimization_barrier((copies, packed))
    all_hidden = swap(copies, "sample")
    map_grads = exchange([map_grad] * chans, chans)
    late, _ = lax.optimization_barrier((hidden, map_grads[1]))
    parts = exchange(
        call(run(second_kernel), [piece] * chans, [second_w, late], patches, "second", 2.8), chans
    )
    full_map_grad = call(run(join_kernel), [((full, CELLS), BF16)], map_grads, name="join")[0]
    full_map_grad, all_hidden = lax.optimization_barrier((full_map_grad, all_hidden))
    all_map_grad = swap(full_map_grad.reshape(samples, outs, CELLS), "sample")
    second_out = sum(p.astype(F32) for p in parts).astype(BF16)
    second_grad = grad(all_hidden, packed, ins, ins)
    first_grad = grad(packed, all_map_grad, ins, 0)
    return (
        second_out[None],
        first_grad.transpose(2, 0, 1),
        second_grad.transpose(2, 0, 1),
    )


def half(rows):
    return pl.ds(pl.multiple_of((lax.axis_index("sample") & 1) * rows, rows), rows)


def far(step, rows):
    chip = (lax.axis_index("sample") >> 1) ^ step
    return pl.ds(pl.multiple_of(chip * rows, rows), rows)


def cells_kernel(chans, v_ref, *outs):
    for j, out in enumerate(outs):
        out[...] = v_ref[block(j, chans, out.shape[0]), :]


def input_kernel(chans, w_ref, *refs):
    parts, (x, *outs), scratch = refs[:chans], refs[chans:-2], refs[-2:]
    for j, part in enumerate(parts):
        x[:, block(chans - j, chans, part.shape[1])] = part[...]
    conv_part(chans, w_ref, x[...], outs, *scratch)


def pieces_kernel(hidden, x, full, out):
    rows = x.shape[0]
    for chip in range(out.shape[0]):
        out[chip, :rows, :] = hidden[...]
        out[chip, rows : 2 * rows, :] = x[...]
        out[chip, 2 * rows :, :] = full[chip * rows : (chip + 1) * rows, :]


def gate_kernel(chans, hidden_grad, *refs):
    parts, (hidden_ref, keep, give, both) = refs[:chans], refs[chans:]
    total = parts[0][...].astype(F32)
    for j in range(1, chans):
        total = total + parts[j][...].astype(F32)
    first_map = total.astype(BF16).astype(F32)
    gate = 1.0 / (1.0 + jnp.exp(-first_map))
    hidden_ref[...] = (first_map * gate).astype(BF16)
    both[...] = (hidden_grad[...] * gate * (1.0 + first_map * (1.0 - gate))).astype(BF16)
    rows = keep.shape[0]
    keep[...] = both[half(rows), :]
    other = pl.multiple_of((1 - (lax.axis_index("sample") & 1)) * rows, rows)
    give[...] = both[pl.ds(other, rows), :]


def stack_kernel(top, bottom, out):
    rows = top.shape[0]
    out[:rows, :] = top[...]
    out[rows:, :] = bottom[...]


def route_kernel(chans, *refs):
    parts, outs, full = refs[:chans], refs[chans:-1], refs[-1]
    rows = outs[0].shape[0]
    join_kernel(chans, *parts, full)
    for step, out in enumerate(outs):
        out[...] = full[far(step, rows), :]


def total_kernel(*refs):
    *parts, out = refs
    total = parts[0][...].astype(F32)
    for part in parts[1:]:
        total = total + part[...].astype(F32)
    out[...] = total.astype(BF16)


def second_grad_kernel(mine, other, *rest):
    rows, ins = rest[0].shape[1:]
    start = pl.multiple_of(2 * ins + (lax.axis_index("sample") & 1) * rows, rows)
    pairs = []
    for chip in range(mine.shape[0]):
        for v in (mine, other):
            pairs.append((v[chip, :ins, :], v[chip, pl.ds(start, rows), :]))
    grad_sum(pairs, *rest)


def first_grad_kernel(steps, mine, other, *refs):
    count = len(steps)
    maps, begin, rest = refs[:count], refs[count:-3], refs[-3:]
    rows, ins = rest[0].shape[1:]
    pairs = []
    for step, g in zip(steps, maps):
        chip = (lax.axis_index("sample") >> 1) ^ step
        for core, v in enumerate((mine, other)):
            at = core * rows
            pairs.append((v[chip, ins : 2 * ins, :], g[at : at + rows, :]))
    grad_sum(pairs, *rest, *begin)


def body(samples, chans, snapshots, first_weight, second_weight, cotangent):
    ins = first_weight.shape[0]
    full = snapshots.shape[1]
    outs = full // samples
    chips = samples // 2
    run = lambda kernel: functools.partial(kernel, chans)
    first_w = first_weight.transpose(1, 0, 2)
    second_w = second_weight.transpose(1, 0, 2)
    patches = [pltpu.VMEM((27 * ins, CELLS), BF16), pltpu.VMEM((full, CELLS), BF16)]
    piece = ((ins, CELLS), BF16)
    hop = lambda v, step: lax.ppermute(v, "sample", [(s, s ^ step) for s in range(samples)])

    def chip_hops(parts):
        return [parts[0]] + [hop(parts[d], 2 * d) for d in range(1, chips)]

    cells = call(
        run(cells_kernel), [((ins, CELLS // chans), BF16)] * chans, [snapshots[0]], (), "cells", 0.5
    )
    cells = exchange(cells, chans)
    cots = exchange([cotangent[0]] * chans, chans)
    cots[1], *cells = lax.optimization_barrier((cots[1], *cells))
    x, *parts = call(
        run(input_kernel), [piece] * (chans + 1), [first_w] + cells, patches, "first", 1.0
    )
    parts = exchange(parts, chans)
    full_cot = call(run(join_kernel), [((full, CELLS), BF16)], cots, (), "join", 0.5)[0]
    hidden_grad = call(
        spread_kernel, [((ins, CELLS), F32)], [second_w, full_cot], (), "spread", 1.5
    )[0]
    hidden, keep, give = call(
        run(gate_kernel),
        [piece, ((outs, CELLS), BF16), ((outs, CELLS), BF16)],
        [hidden_grad] + parts,
        [pltpu.VMEM((ins, CELLS), BF16)],
        "gate",
        0.9,
    )
    got = hop(give, 1)
    map_grad = call(stack_kernel, [piece], [keep, got], (), "stack", 0.3)[0]
    map_grads = exchange([map_grad] * chans, chans)
    parts = exchange(
        call(run(second_kernel), [piece] * chans, [second_w, hidden], patches, "second", 0.9), chans
    )
    pieces = call(
        pieces_kernel,
        [((chips, 3 * ins, CELLS), BF16)],
        [hidden, x, full_cot],
        (),
        "pieces",
        0.8,
    )[0]
    pieces, got = lax.optimization_barrier((pieces, got))
    cores = [list(range(core, samples, 2)) for core in (0, 1)]
    pieces = lax.all_to_all(pieces, "sample", 0, 0, axis_index_groups=cores, tiled=True)
    routed = call(run(route_kernel), [piece] * chips, map_grads, patches[1:], "route", 15.0)
    map_grads = chip_hops(routed)
    pieces = [pieces, hop(pieces, 1)]
    def grad_call(kernel, args, count):
        scratch = [
            pltpu.VMEM((9 * outs, count * CELLS), BF16),
            pltpu.VMEM((3 * ins, count * CELLS), BF16),
        ]
        us = 0.3
        return call(kernel, [((27, outs, ins), F32)], args, scratch, "grad", us)[0]

    second_grad = grad_call(second_grad_kernel, pieces, samples)
    second_grad, *parts = lax.optimization_barrier((second_grad, *parts))
    second_out = call(total_kernel, [piece], parts, (), "total", 0.1)[0]
    first_grad = []
    for steps in (range(chips - 1), [chips - 1]):
        args = pieces + [map_grads[d] for d in steps] + first_grad
        kernel = functools.partial(first_grad_kernel, tuple(steps))
        first_grad = [grad_call(kernel, args, 2 * len(steps))]
    first_grad = first_grad[0]
    return (
        second_out[None],
        first_grad.transpose(2, 0, 1),
        second_grad.transpose(2, 0, 1),
    )


def solution(mesh):
    placed = (
        P("sample", None, "chan"),
        P("chan", None, None),
        P("chan", None, None),
        P("sample", "chan", None),
    )
    samples, chans = mesh.shape["sample"], mesh.shape["chan"]
    square = samples == 2 * chans and chans in (2, 4)
    return jax.shard_map(
        functools.partial(body if square else plain_body, samples, chans),
        mesh=mesh,
        in_specs=placed,
        out_specs=(P("sample", "chan", None), P("chan", None, "sample"), P("chan", None, "sample")),
        check_vma=False,
    )
```
